256 devices in a mesh: shard: 32 (over x_lo, z, core), tensor: 4 (over y), section: 2 (over x_hi).
Axes of the slice: x: 4 (x_hi: 2, x_lo: 2; x = x_hi * 2 + x_lo), y: 4, z: 8, core: 2. Of those that a mesh axis runs over, the one named last changes fastest.
Arguments:
- grads: bfloat16 [32, 4, 3072, 768], P('shard', 'section', 'tensor'), may hold values from -120 to 120
- weights: bfloat16 [4, 3072, 768], P('section', 'tensor'), may hold values from -3 to 3
- basis: float32 [4, 768, 256], P('section'), may hold values from -6 to 6
- first_moment: float32 [4, 3072, 256], P('section', ('tensor', 'shard')), may hold values from -6 to 6
- second_moment: float32 [4, 3072, 256], P('section', ('tensor', 'shard')), may hold values from 0.1 to 4
Outputs:
- weights_next: bfloat16 [4, 3072, 768], P('section', 'tensor')
- basis_next: float32 [4, 768, 256], P('section')
- moment_one: float32 [4, 3072, 256], P('section', ('tensor', 'shard'))
- moment_two: float32 [4, 3072, 256], P('section', ('tensor', 'shard'))
The draws below stay inside these ranges and needn't reach their ends.
All inputs are finite; a program needn't handle non-finite values.
Results may differ from the reference program's by a relative error of at most 0.0004.
Values may be sent and summed in bfloat16 or wider, within the bound.
A program may use at most 64 MiB of HBM per device.

```python
import math
import jax
import jax.numpy as jnp
from jax import lax

D = 768
FF = 3072
RANK = 256
NS_ITERS = 3
STEP = 1000
LAYERS = 4
SHARDS = 32
ROWS_DEV = 24


def draw_grads(key, part):
    subkeys = jax.random.split(jax.random.fold_in(key, 17), 4)
    full_shape = (SHARDS, LAYERS, FF, D)
    base_draw = jnp.clip(jax.random.normal(subkeys[0], full_shape, jnp.float32), -6.0, 6.0)
    row_scale = jnp.exp(jax.random.uniform(subkeys[1], (1, LAYERS, FF, 1), jnp.float32) * math.log(10.0))
    column_scale = jnp.exp(jax.random.uniform(subkeys[3], (1, LAYERS, 1, D), jnp.float32) * math.log(10.0))
    pairing = jax.random.permutation(subkeys[2], SHARDS)
    blocks = jnp.arange(FF) // ROWS_DEV % SHARDS
    spike_gain = jnp.where(blocks[None, :] == pairing[:, None], 4.0, 1.0)
    values = 0.05 * base_draw * row_scale * column_scale * spike_gain[:, None, :, None]
    return values.astype(jnp.bfloat16)


def block_levels(rng, dims, pieces, smallest, top_value):
    factor_of = 1.0
    for position, blocks in pieces:
        steps = jax.random.uniform(jax.random.fold_in(jax.random.fold_in(rng, 6), position), (blocks,), jnp.float32, smallest / len(pieces), top_value / len(pieces))
        factor_of = factor_of * jnp.repeat(jnp.exp(steps), dims[position] // blocks).reshape((-1,) + (1,) * (len(dims) - 1 - position))
    return factor_of


def bell_draw(rng, extent, deviation, most, shards=(), held_as=jnp.bfloat16):
    gain = block_levels(rng, extent, shards, -0.22, 0.18) if shards else 1.0
    drawn = jax.random.normal(rng, extent, jnp.float32) * deviation * gain
    return jnp.minimum(jnp.maximum(drawn, -most), most).astype(held_as)


def setup_inputs(seed: int = 0) -> dict:
    splits = jax.random.split(jax.random.key(seed), 6)
    return {
        "grads": draw_grads(jax.random.fold_in(splits[5], 71), 0),
        "weights": bell_draw(splits[1], (LAYERS, FF, D), 0.5, 3.0, ((0, 2), (1, 4))),
        "basis": bell_draw(splits[2], (LAYERS, D, RANK), 1.0, 6.0, ((0, 2),), jnp.float32),
        "first_moment": bell_draw(splits[3], (LAYERS, FF, RANK), 1.0, 6.0, ((0, 2), (1, 128)), jnp.float32),
        "second_moment": jnp.clip(jnp.exp(math.log(4.0) - 3.6888794 * jax.random.uniform(splits[4], (LAYERS, FF, RANK), jnp.float32) ** block_levels(splits[4], (LAYERS, FF, RANK), ((0, 2), (1, 128)), -0.2, 0.2)), 0.1, 4.0),
    }


learn_rate = 0.5
galore_scale = 0.25
beta_one = 0.9
beta_two = 0.999
adam_eps = 1e-08
norm_eps = 1e-07
coeff_a = 3.4445
coeff_b = -4.775
coeff_c = 2.0315
highest = lax.Precision.HIGHEST

def newton_step(iterate, gram_matrix):
    squared = jnp.einsum('lrs,lst->lrt', gram_matrix, gram_matrix, precision=highest)
    mixing = coeff_b * gram_matrix + coeff_c * squared
    return coeff_a * iterate + jnp.einsum('ldr,lrs->lds', iterate, mixing, precision=highest)

def adam_direction(reduced, first_moment, second_moment):
    moment_one = beta_one * first_moment + (1.0 - beta_one) * reduced
    moment_two = beta_two * second_moment + (1.0 - beta_two) * reduced * reduced
    corrected_one = moment_one / (1.0 - beta_one ** STEP)
    corrected_two = moment_two / (1.0 - beta_two ** STEP)
    return (moment_one, moment_two, corrected_one / (jnp.sqrt(corrected_two) + adam_eps))

def reference(grads, weights, basis, first_moment, second_moment):

    def accumulate(running, block_grad):
        return (running + block_grad.astype(jnp.float32), None)
    summed, leftover = lax.scan(accumulate, jnp.zeros(weights.shape, jnp.float32), grads)
    scale_factor = D ** (-0.5)
    projected = jnp.einsum('lfd,ldr->lfr', summed, basis, precision=highest)
    reduced = scale_factor * projected
    moment_one, moment_two, direction = adam_direction(reduced, first_moment, second_moment)
    update = jnp.einsum('lfr,ldr->lfd', direction, basis, precision=highest)
    factor = learn_rate * galore_scale * scale_factor
    weights_next = (weights.astype(jnp.float32) - factor * update).astype(jnp.bfloat16)
    power = jnp.einsum('lfd,lfr->ldr', summed, projected, precision=highest)
    norms = jnp.sqrt(lax.optimization_barrier(jnp.sum(power * power, axis=(1, 2))))
    iterate = power / (norms + norm_eps)[:, None, None]
    for sweep in range(NS_ITERS):
        gram_matrix = jnp.einsum('ldr,lds->lrs', iterate, iterate, precision=highest)
        iterate = newton_step(iterate, gram_matrix)
    basis_next = D ** 0.5 * iterate
    return (weights_next, basis_next, moment_one, moment_two)
```

```python
import jax
import jax.numpy as jnp
from jax import lax
from jax.experimental import pallas as pl
from jax.experimental.pallas import tpu as pltpu
from jax.sharding import PartitionSpec as P

NS_ITERS = 3
STEP = 1000

learn_rate = 0.5
galore_scale = 0.25
beta_one = 0.9
beta_two = 0.999
adam_eps = 1e-08
norm_eps = 1e-07
coeff_a = 3.4445
coeff_b = -4.775
coeff_c = 2.0315

f32 = jnp.float32
bf16 = jnp.bfloat16
MESH = pl.DeviceIdType.MESH

NX, NZ, NY = 2, 8, 4
Z_FAR = (4, 3, 5, 2, 6, 1, 7)
Z_NEAR = (1, 7, 2, 6, 3, 5, 4)


def halves(value):
    high = value.astype(bf16)
    return high, (value - high.astype(f32)).astype(bf16)


def mm(a, b):
    return jnp.dot(a, b, preferred_element_type=f32)


def mm3(a, b):
    (ah, al), (bh, bl) = a, b
    return mm(ah, bh) + (mm(ah, bl) + mm(al, bh))


def adam(reduced, first, second):
    one = beta_one * first + (1.0 - beta_one) * reduced
    two = beta_two * second + (1.0 - beta_two) * reduced * reduced
    corrected_one = one / (1.0 - beta_one**STEP)
    corrected_two = two / (1.0 - beta_two**STEP)
    return one, two, corrected_one / (jnp.sqrt(corrected_two) + adam_eps)


def kernel(
    grads, weights, basis, first, second,
    wn, bn, o1, o2,
    g, gs, gt, b, bh, bl, bt, w, p, ps, xr, rz, pf, pfh, pfl, df, mo, mres,
    pw, r1, s2, r2, z2, pwf,
    lsem, sps, spr, ses, ser, xs, xrr, zs, zr, ags, agr, fws, drs, drr,
    p1s, p1r, p2s, p2r, q2s, q2r, q1s, q1r, ws, wr, bs, br,
):
    s = lax.axis_index("shard")
    y = lax.axis_index("tensor")
    x, z, c = s // 16, (s // 2) % 8, s % 2
    other = 1 - c
    ox = 1 - x
    width, rank = b.shape[1], b.shape[2]
    scale = width ** (-0.5)

    def at(dx=0, dz=0, dy=0, dc=0):
        return {
            "shard": (((x + dx) % NX) * NZ + (z + dz) % NZ) * 2 + (c + dc) % 2,
            "tensor": (y + dy) % NY,
        }

    sib = at(dc=1)
    xpeer = at(dx=1)

    def copy(src, dst, ss, rs, dev):
        return pltpu.make_async_remote_copy(
            src_ref=src, dst_ref=dst, send_sem=ss, recv_sem=rs, device_id=dev, device_id_type=MESH
        )

    barrier = pltpu.get_barrier_semaphore()
    peers = [sib]
    peers += [at(dx=dx, dy=dy) for dx in range(NX) for dy in range(NY) if (dx, dy) != (0, 0)]
    peers += [at(dz=dz) for dz in range(1, NZ)]
    for dev in peers:
        pl.semaphore_signal(barrier, 1, device_id=dev, device_id_type=MESH)

    loads = [
        pltpu.make_async_copy(basis.at[other], b.at[other], lsem.at[0]),
        pltpu.make_async_copy(grads.at[0, other], g.at[other], lsem.at[1]),
        pltpu.make_async_copy(basis.at[c], b.at[c], lsem.at[2]),
        pltpu.make_async_copy(grads.at[0, c], g.at[c], lsem.at[3]),
        pltpu.make_async_copy(first.at[c], mo.at[0, c], lsem.at[4]),
        pltpu.make_async_copy(second.at[c], mo.at[1, c], lsem.at[5]),
        pltpu.make_async_copy(weights.at[c], w, lsem.at[6]),
    ]
    for load in loads:
        load.start()

    def project(layer, column):
        rows = pl.ds(pl.multiple_of(column * 384, 384), 384)
        left = g[layer, rows, :]
        out = mm(left, bh[layer]) + mm(left, bl[layer])
        p[layer, pl.ds(column * 8, 8)] = out.reshape(8, 48, rank)

    def split_basis(layer):
        high, low = halves(b[layer])
        bh[layer] = high
        bl[layer] = low

    loads[0].wait()
    split_basis(other)
    loads[1].wait()
    project(other, ox)
    project(other, x)
    pl.semaphore_wait(barrier, len(peers))

    order = [(1, dz) for dz in Z_FAR + (0,)] + [(0, dz) for dz in Z_FAR + (0,)]

    def block(dx, dz):
        return ((x + dx) % NX) * NZ + (z + dz) % NZ

    to_sib = []
    for k, (dx, dz) in enumerate(order):
        n = block(dx, dz)
        to_sib.append(copy(p.at[other, n], ps.at[n], sps.at[k], spr.at[k], sib))
        to_sib[-1].start()
    extras = [
        copy(first.at[other], mo.at[0, c], ses.at[1], ser.at[1], sib),
        copy(second.at[other], mo.at[1, c], ses.at[2], ser.at[2], sib),
        copy(g.at[other], gs, ses.at[0], ser.at[0], sib),
    ]
    for item in extras:
        item.start()

    loads[2].wait()
    split_basis(c)
    loads[3].wait()
    project(c, ox)
    project(c, x)

    def own_block(k):
        dx, dz = order[k]
        n = block(dx, dz)
        to_sib[k].wait_recv()
        p[c, n] = p[c, n] + ps[n]
        return n

    over_x = []
    for k in range(8):
        n = own_block(k)
        slot = (z + order[k][1]) % NZ
        over_x.append(copy(p.at[c, n], xr.at[slot], xs.at[k], xrr.at[k], xpeer))
        over_x[-1].start()
    over_z = []
    for k in range(8):
        n = own_block(8 + k)
        dz = order[8 + k][1]
        slot = (z + dz) % NZ
        over_x[k].wait_recv()
        if dz:
            p[c, n] = p[c, n] + xr[slot]
            over_z.append(copy(p.at[c, n], rz.at[z], zs.at[k], zr.at[z], at(dz=dz)))
            over_z[-1].start()
        else:
            rz[z] = p[c, n] + xr[slot]

    copy(g.at[other], gs, ses.at[0], ser.at[0], sib).wait_recv()
    gt[0] = g[c].T
    gt[1] = gs[...].T
    bt[0] = bh[c].T
    bt[1] = bl[c].T

    total = rz[z]
    for dz in Z_NEAR:
        src = (z + dz) % NZ
        copy(rz.at[src], rz.at[src], zs.at[0], zr.at[src], sib).wait_recv()
        total = total + rz[src]
    mine = x * NZ + z
    pf[mine] = total

    gather = []
    for k, dz in enumerate(Z_NEAR):
        gather.append(copy(pf.at[mine], pf.at[mine], ags.at[k], agr.at[mine], at(dz=dz)))
        gather[-1].start()
    gather.append(copy(pf.at[mine], pf.at[mine], ags.at[7], agr.at[mine], xpeer))
    gather[-1].start()

    extras[0].wait_recv()
    extras[1].wait_recv()
    for load in loads[4:6]:
        load.wait()
    one, two, direction = adam(
        scale * total, mo[0].reshape(48, rank), mo[1].reshape(48, rank)
    )
    mres[0] = one.reshape(2, 24, rank)
    mres[1] = two.reshape(2, 24, rank)
    o1[c] = mres[0, c]
    o2[c] = mres[1, c]
    df[mine] = direction
    finish = [
        copy(mres.at[0, other], o1.at[c], ses.at[3], ser.at[3], sib),
        copy(mres.at[1, other], o2.at[c], ses.at[4], ser.at[4], sib),
        copy(df.at[mine], df.at[mine], drs.at[14], drr.at[mine], xpeer),
    ]
    for item in finish:
        item.start()

    forward = []
    for k, dz in enumerate(Z_NEAR):
        src = x * NZ + (z + dz) % NZ
        copy(pf.at[src], pf.at[src], ags.at[0], agr.at[src], sib).wait_recv()
        forward.append(copy(pf.at[src], pf.at[src], fws.at[k], agr.at[src], xpeer))
        forward[-1].start()
    for dz in (0,) + Z_NEAR:
        src = ox * NZ + (z + dz) % NZ
        copy(pf.at[src], pf.at[src], ags.at[0], agr.at[src], sib).wait_recv()

    theirs = ox * NZ + z
    copy(df.at[theirs], df.at[theirs], drs.at[0], drr.at[theirs], sib).wait_recv()
    directions = []
    for k, dz in enumerate(Z_NEAR):
        for j, n in enumerate((mine, theirs)):
            directions.append(copy(df.at[n], df.at[n], drs.at[2 * k + j], drr.at[n], at(dz=dz)))
            directions[-1].start()

    high, low = halves(pf[...].reshape(768, rank))
    pfh[...] = high
    pfl[...] = low
    over_q = []
    me_q = x * NY + y
    for dx in (1, 0):
        tx = (x + dx) % NX
        rows = pl.ds(pl.multiple_of(tx * 384, 384), 384)
        own, near = gt[0, rows, :], gt[1, rows, :]
        out = (mm(own, pfh[...]) + mm(near, pfh[...])) + (mm(own, pfl[...]) + mm(near, pfl[...]))
        pw[pl.ds(tx * NY, NY)] = out.reshape(NY, 96, rank)
        for dy in (2, 1, 3, 0):
            if (dx, dy) == (0, 0):
                r1[me_q] = pw[me_q]
                continue
            k = dx * NY + dy
            n = tx * NY + (y + dy) % NY
            over_q.append(copy(pw.at[n], r1.at[me_q], p1s.at[k], p1r.at[me_q], at(dx=dx, dy=dy)))
            over_q[-1].start()

    partial = r1[me_q]
    for dx, dy in ((0, 1), (0, 3), (1, 0), (1, 1), (1, 3), (0, 2), (1, 2)):
        src = ((x + dx) % NX) * NY + (y + dy) % NY
        copy(r1.at[src], r1.at[src], p1s.at[0], p1r.at[src], sib).wait_recv()
        partial = partial + r1[src]
    for t in range(NZ):
        s2[t] = partial[24 * (t // 2) : 24 * (t // 2) + 24, 128 * (t % 2) : 128 * (t % 2) + 128]
    over_z2 = []
    for k, dz in enumerate(Z_FAR):
        over_z2.append(copy(s2.at[(z + dz) % NZ], r2.at[z], p2s.at[k], p2r.at[z], at(dz=dz)))
        over_z2[-1].start()
    piece = s2[z]
    for dz in Z_NEAR:
        src = (z + dz) % NZ
        copy(r2.at[src], r2.at[src], p2s.at[0], p2r.at[src], sib).wait_recv()
        piece = piece + r2[src]
    z2[z] = piece
    gather_z = []
    for k, dz in enumerate(Z_FAR):
        gather_z.append(copy(z2.at[z], z2.at[z], q2s.at[k], q2r.at[z], at(dz=dz)))
        gather_z[-1].start()
    for dz in Z_NEAR:
        src = (z + dz) % NZ
        copy(z2.at[src], z2.at[src], q2s.at[0], q2r.at[src], sib).wait_recv()
    for t in range(NZ):
        pwf[me_q, 24 * (t // 2) : 24 * (t // 2) + 24, 128 * (t % 2) : 128 * (t % 2) + 128] = z2[t]
    gather_q = []
    for dx, dy in ((1, 2), (0, 2), (1, 1), (1, 3), (0, 1), (0, 3), (1, 0)):
        gather_q.append(
            copy(pwf.at[me_q], pwf.at[me_q], q1s.at[dx * NY + dy], q1r.at[me_q], at(dx=dx, dy=dy))
        )
        gather_q[-1].start()

    for dx in range(NX):
        for dz in range(NZ):
            if (dx, dz) not in ((0, 0), (1, 0)):
                src = block(dx, dz)
                copy(df.at[src], df.at[src], drs.at[0], drr.at[src], sib).wait_recv()
    loads[6].wait()
    factor = learn_rate * galore_scale * scale
    to_weights = []
    for k in range(2):
        rows = pl.ds(384 * k, 384)
        dh, dl = halves(df[8 * k : 8 * k + 8].reshape(384, rank))
        update = mm3((dh, dl), (bt[0], bt[1]))
        wn[c, rows, :] = (w[rows, :].astype(f32) - factor * update).astype(bf16)
        to_weights.append(copy(wn.at[c, rows], wn.at[c, rows], ws.at[k], wr.at[k], sib))
        to_weights[-1].start()

    for dx, dy in ((0, 1), (0, 3), (1, 0), (1, 1), (1, 3), (0, 2), (1, 2)):
        src = ((x + dx) % NX) * NY + (y + dy) % NY
        copy(pwf.at[src], pwf.at[src], q1s.at[0], q1r.at[src], sib).wait_recv()

    power = pwf[...].reshape(768, rank)
    norm = jnp.sqrt(jnp.sum(power * power))
    iterate = power * (1.0 / (norm + norm_eps))
    it = halves(iterate)
    gram = mm3((it[0].T, it[1].T), it)
    diagonal = (
        lax.broadcasted_iota(jnp.int32, (rank, rank), 0)
        == lax.broadcasted_iota(jnp.int32, (rank, rank), 1)
    )
    mix = None
    for sweep in range(NS_ITERS):
        gh = halves(gram)
        step = coeff_b * gram + coeff_c * mm3(gh, gh)
        step = step + jnp.where(diagonal, coeff_a, 0.0)
        sh = halves(step)
        mix = sh if mix is None else halves(mm3(mix, sh))
        if sweep < NS_ITERS - 1:
            gram = mm3(halves(mm3(gh, sh)), sh)
    to_basis = []
    for k in range(2):
        rows = pl.ds(384 * k, 384)
        left = halves(iterate[384 * k : 384 * k + 384])
        bn[c, rows, :] = width**0.5 * mm3(left, mix)
        to_basis.append(copy(bn.at[c, rows], bn.at[c, rows], bs.at[k], br.at[k], sib))
        to_basis[-1].start()

    for item in finish[:2] + to_weights + to_basis:
        item.wait_recv()
    for group in (
        to_sib, extras, over_x, over_z, gather, finish, forward, directions, over_q, over_z2,
        gather_z, gather_q, to_weights, to_basis,
    ):
        for item in group:
            item.wait_send()


def body(grads, weights, basis, first, second):
    layers, width, rank = basis.shape
    any_spec = pl.BlockSpec(memory_space=pl.ANY)
    vmem_spec = pl.BlockSpec(memory_space=pltpu.VMEM)
    dma = pltpu.SemaphoreType.DMA
    return pl.pallas_call(
        kernel,
        out_shape=(
            jax.ShapeDtypeStruct(weights.shape, bf16),
            jax.ShapeDtypeStruct(basis.shape, f32),
            jax.ShapeDtypeStruct(first.shape, f32),
            jax.ShapeDtypeStruct(second.shape, f32),
        ),
        in_specs=[any_spec] * 5,
        out_specs=[vmem_spec] * 4,
        scratch_shapes=[
            pltpu.VMEM((2, 768, 768), bf16),
            pltpu.VMEM((768, 768), bf16),
            pltpu.VMEM((2, 768, 768), bf16),
            pltpu.VMEM((2, 768, 256), f32),
            pltpu.VMEM((2, 768, 256), bf16),
            pltpu.VMEM((2, 768, 256), bf16),
            pltpu.VMEM((2, 256, 768), bf16),
            pltpu.VMEM((768, 768), bf16),
            pltpu.VMEM((2, 16, 48, 256), f32),
            pltpu.VMEM((16, 48, 256), f32),
            pltpu.VMEM((8, 48, 256), f32),
            pltpu.VMEM((8, 48, 256), f32),
            pltpu.VMEM((16, 48, 256), f32),
            pltpu.VMEM((768, 256), bf16),
            pltpu.VMEM((768, 256), bf16),
            pltpu.VMEM((16, 48, 256), f32),
            pltpu.VMEM((2, 2, 24, 256), f32),
            pltpu.VMEM((2, 2, 24, 256), f32),
            pltpu.VMEM((8, 96, 256), f32),
            pltpu.VMEM((8, 96, 256), f32),
            pltpu.VMEM((8, 24, 128), f32),
            pltpu.VMEM((8, 24, 128), f32),
            pltpu.VMEM((8, 24, 128), f32),
            pltpu.VMEM((8, 96, 256), f32),
            dma((7,)),
            dma((16,)), dma((16,)),
            dma((5,)), dma((5,)),
            dma((8,)), dma((8,)),
            dma((8,)), dma((8,)),
            dma((8,)), dma((16,)), dma((7,)),
            dma((15,)), dma((16,)),
            dma((8,)), dma((8,)),
            dma((7,)), dma((8,)),
            dma((7,)), dma((8,)),
            dma((8,)), dma((8,)),
            dma((2,)), dma((2,)),
            dma((2,)), dma((2,)),
        ],
        name="galore_step",
        compiler_params=pltpu.CompilerParams(
            collective_id=0, has_side_effects=True, vmem_limit_bytes=56 << 20
        ),
    )(grads, weights, basis, first, second)


def solution(mesh):
    return jax.shard_map(
        body,
        mesh=mesh,
        in_specs=(
            P("shard", "section", "tensor", None),
            P("section", "tensor", None),
            P("section", None, None),
            P("section", ("tensor", "shard"), None),
            P("section", ("tensor", "shard"), None),
        ),
        out_specs=(
            P("section", "tensor", None),
            P("section", None, None),
            P("section", ("tensor", "shard"), None),
            P("section", ("tensor", "shard"), None),
        ),
        check_vma=False,
    )
```

```python
import jax
import jax.numpy as jnp
from jax import lax
from jax.experimental import pallas as pl
from jax.experimental.pallas import tpu as pltpu
from jax.sharding import PartitionSpec as P

NS_ITERS = 3
STEP = 1000

learn_rate = 0.5
galore_scale = 0.25
beta_one = 0.9
beta_two = 0.999
adam_eps = 1e-08
norm_eps = 1e-07
coeff_a = 3.4445
coeff_b = -4.775
coeff_c = 2.0315

f32 = jnp.float32
bf16 = jnp.bfloat16
MESH = pl.DeviceIdType.MESH

NX, NZ, NY = 2, 8, 4
Z_FAR = (4, 3, 5, 2, 6, 1, 7)
Z_NEAR = (1, 7, 2, 6, 3, 5, 4)
Z_VIA_X = (4, 3, 5, 2, 6)
Q_NEAR = ((0, 1), (0, 3), (1, 0), (1, 1), (1, 3), (0, 2), (1, 2))
Q_ALL = ((1, 2), (1, 1), (1, 3), (1, 0), (0, 2), (0, 1), (0, 3))


def halves(value):
    high = value.astype(bf16)
    return high, (value - high.astype(f32)).astype(bf16)


def mm(a, b):
    return jnp.dot(a, b, preferred_element_type=f32)


def mm3(a, b):
    (ah, al), (bh, bl) = a, b
    return mm(ah, bh) + (mm(ah, bl) + mm(al, bh))


def adam(reduced, first, second):
    one = beta_one * first + (1.0 - beta_one) * reduced
    two = beta_two * second + (1.0 - beta_two) * reduced * reduced
    corrected_one = one / (1.0 - beta_one**STEP)
    corrected_two = two / (1.0 - beta_two**STEP)
    return one, two, corrected_one / (jnp.sqrt(corrected_two) + adam_eps)


class Flow:
    def __init__(self, me, log, src, dst, send, recv, rel):
        away = {
            "shard": (((me[0] + rel[0]) % NX) * NZ + (me[1] + rel[1]) % NZ) * 2 + (me[3] + rel[3]) % 2,
            "tensor": (me[2] + rel[2]) % NY,
        }
        sizes = (NX, NZ, NY, 2)
        back = tuple(m if r == 0 else (m - r + n) % n for m, r, n in zip(me, rel, sizes))
        self.out = pltpu.make_async_remote_copy(
            src_ref=src, dst_ref=dst(*me), send_sem=send, recv_sem=recv(*me), device_id=away, device_id_type=MESH
        )
        self.back = pltpu.make_async_remote_copy(
            src_ref=dst(*back), dst_ref=dst(*back), send_sem=send, recv_sem=recv(*back),
            device_id=away, device_id_type=MESH,
        )
        self.log = log
        self.waiting = True
        log.append(self)
        self.out.start()

    def recv(self):
        self.back.wait_recv()
        self.waiting = False

    def done(self):
        if self.waiting:
            self.recv()
        self.out.wait_send()


def kernel(
    grads, weights, basis, first, second,
    wn, bn, o1, o2,
    g, gs, gt, b, bh, bl, bt, w, p, ps, xr, rz, pf, pfh, pfl, df, mo, mres,
    pwa, pwb, ra, rb, sa, sb, ra2, rb2, zb, fa, fb,
    lsem, sps, spr, ses, ser, xs, xrr, zs, zr, ags, agr, fws, drs, drr,
    bas, bar_, bbs, bbr, sas, sar, sbs, sbr, gas, gar, gbs, gbr, has, har, hbs, hbr, ws, wr, bs, br,
    stop=99,
):
    s = lax.axis_index("shard")
    y = lax.axis_index("tensor")
    x, z, c = s // 16, (s // 2) % 8, s % 2
    me = (x, z, y, c)
    other = 1 - c
    ox = 1 - x
    width, rank = b.shape[1], b.shape[2]
    scale = width ** (-0.5)
    log = []
    SIB, XP = (0, 0, 0, 1), (1, 0, 0, 0)

    def send(src, dst, ss, rs, rel):
        return Flow(me, log, src, dst, ss, rs, rel)

    def finish():
        for item in log:
            item.done()

    barrier = pltpu.get_barrier_semaphore()
    peers = [SIB]
    peers += [(dx, 0, dy, 0) for dx in range(NX) for dy in range(NY) if (dx, dy) != (0, 0)]
    peers += [(0, dz, 0, 0) for dz in range(1, NZ)] + [(1, 1, 0, 0), (1, 7, 0, 0)]
    for dx, dz, dy, dc in peers:
        dev = {"shard": (((x + dx) % NX) * NZ + (z + dz) % NZ) * 2 + (c + dc) % 2, "tensor": (y + dy) % NY}
        pl.semaphore_signal(barrier, 1, device_id=dev, device_id_type=MESH)

    loads = [
        pltpu.make_async_copy(basis.at[other], b.at[other], lsem.at[0]),
        pltpu.make_async_copy(grads.at[0, other], g.at[other], lsem.at[1]),
        pltpu.make_async_copy(basis.at[c], b.at[c], lsem.at[2]),
        pltpu.make_async_copy(grads.at[0, c], g.at[c], lsem.at[3]),
        pltpu.make_async_copy(first.at[c], mo.at[0, c], lsem.at[4]),
        pltpu.make_async_copy(second.at[c], mo.at[1, c], lsem.at[5]),
        pltpu.make_async_copy(weights.at[c], w, lsem.at[6]),
    ]
    for load in loads:
        load.start()

    def project(layer, column):
        rows = pl.ds(pl.multiple_of(column * 384, 384), 384)
        left = g[layer, rows, :]
        out = mm(left, bh[layer]) + mm(left, bl[layer])
        p[layer, pl.ds(column * 8, 8)] = out.reshape(8, 48, rank)

    def split_basis(layer):
        high, low = halves(b[layer])
        bh[layer] = high
        bl[layer] = low

    loads[0].wait()
    split_basis(other)
    loads[1].wait()
    project(other, ox)
    project(other, x)
    loads[2].wait()
    split_basis(c)
    loads[3].wait()
    project(c, ox)
    project(c, x)
    if stop == -1:
        for load in loads[4:]:
            load.wait()
        pl.semaphore_wait(barrier, len(peers))
        return
    pl.semaphore_wait(barrier, len(peers))

    order = [(0, 1), (0, 7)] + [(1, dz) for dz in Z_VIA_X + (1, 7, 0)] + [(0, dz) for dz in Z_VIA_X + (0,)]

    def block(xx, zz, dx, dz):
        return ((xx + dx) % NX) * NZ + (zz + dz) % NZ

    to_sib = {}
    for k, (dx, dz) in enumerate(order):
        to_sib[dx, dz] = send(
            p.at[other, block(x, z, dx, dz)],
            lambda x, z, y, c, dx=dx, dz=dz: ps.at[block(x, z, dx, dz)],
            sps.at[k], lambda *_, k=k: spr.at[k], SIB,
        )
    first_in = send(first.at[other], lambda x, z, y, c: mo.at[0, c], ses.at[1], lambda *_: ser.at[1], SIB)
    second_in = send(second.at[other], lambda x, z, y, c: mo.at[1, c], ses.at[2], lambda *_: ser.at[2], SIB)
    grads_in = send(g.at[other], lambda *_: gs, ses.at[0], lambda *_: ser.at[0], SIB)

    if stop == 1:
        for load in loads[4:]:
            load.wait()
        return finish()

    def own_block(dx, dz):
        n = block(x, z, dx, dz)
        to_sib[dx, dz].recv()
        p[c, n] = p[c, n] + ps[n]
        return n

    def to_owner(n, dx, dz, k):
        return send(
            p.at[c, n], lambda x, z, y, c: rz.at[dx, z], zs.at[k], lambda x, z, y, c: zr.at[dx, z], (dx, dz, 0, 0)
        )

    def to_column(dz, k):
        n = own_block(1, dz)
        return send(
            p.at[c, n], lambda x, z, y, c: xr.at[(z + dz) % NZ], xs.at[k], lambda *_: xrr.at[k], XP
        )

    over_z = {}
    for k, dz in enumerate((1, 7)):
        over_z[0, dz] = to_owner(own_block(0, dz), 0, dz, k)
    over_x = {dz: to_column(dz, k) for k, dz in enumerate(Z_VIA_X)}
    for k, dz in enumerate((1, 7)):
        over_z[1, dz] = to_owner(own_block(1, dz), 1, dz, 2 + k)
    over_x[0] = to_column(0, 7)
    if stop == 2:
        for load in loads[4:]:
            load.wait()
        return finish()
    for k, dz in enumerate(Z_VIA_X):
        n = own_block(0, dz)
        over_x[dz].recv()
        p[c, n] = p[c, n] + xr[(z + dz) % NZ]
        over_z[0, dz] = to_owner(n, 0, dz, 4 + k)
    mine = own_block(0, 0)
    if stop == 3:
        for load in loads[4:]:
            load.wait()
        return finish()

    grads_in.recv()
    gt[0] = g[c].T
    gt[1] = gs[...].T
    bt[0] = bh[c].T
    bt[1] = bl[c].T
    if stop == 4:
        for load in loads[4:]:
            load.wait()
        return finish()

    total = p[c, mine]
    for dx, dz in ((0, 1), (0, 7), (1, 1), (1, 7)):
        over_z[dx, dz].recv()
        total = total + rz[dx, (z - dz + NZ) % NZ]
    over_x[0].recv()
    total = total + xr[z]
    for dz in Z_VIA_X:
        over_z[0, dz].recv()
        total = total + rz[0, (z - dz + NZ) % NZ]
    pf[mine] = total
    if stop == 5:
        for load in loads[4:]:
            load.wait()
        return finish()

    piece_at = lambda x, z, y, c: pf.at[x * NZ + z]
    piece_sem = lambda x, z, y, c: agr.at[x * NZ + z]
    gather = {0: send(pf.at[mine], piece_at, ags.at[7], piece_sem, XP)}
    for k, dz in enumerate(Z_NEAR):
        gather[dz] = send(pf.at[mine], piece_at, ags.at[k], piece_sem, (0, dz, 0, 0))

    first_in.recv()
    second_in.recv()
    for load in loads[4:6]:
        load.wait()
    one, two, direction = adam(
        scale * total, mo[0].reshape(48, rank), mo[1].reshape(48, rank)
    )
    mres[0] = one.reshape(2, 24, rank)
    mres[1] = two.reshape(2, 24, rank)
    o1[c] = mres[0, c]
    o2[c] = mres[1, c]
    df[mine] = direction
    send(mres.at[0, other], lambda x, z, y, c: o1.at[c], ses.at[3], lambda *_: ser.at[3], SIB)
    send(mres.at[1, other], lambda x, z, y, c: o2.at[c], ses.at[4], lambda *_: ser.at[4], SIB)
    if stop == 6:
        loads[6].wait()
        return finish()

    gather[0].recv()
    theirs = ox * NZ + z
    forward = [
        send(
            pf.at[theirs], lambda x, z, y, c: pf.at[(1 - x) * NZ + z],
            fws.at[5 + k], lambda x, z, y, c: agr.at[(1 - x) * NZ + z], (0, dz, 0, 0),
        )
        for k, dz in enumerate((1, 7))
    ]
    for dz in (1, 7):
        gather[dz].recv()
    for k, dz in enumerate((2, 6, 3, 5, 4)):
        gather[dz].recv()
        forward.append(send(
            pf.at[x * NZ + (z - dz + NZ) % NZ],
            lambda x, z, y, c, dz=dz: pf.at[x * NZ + (z - dz + NZ) % NZ],
            fws.at[k],
            lambda x, z, y, c, dz=dz: agr.at[x * NZ + (z - dz + NZ) % NZ],
            XP,
        ))
    directions = [
        send(
            df.at[mine], lambda x, z, y, c: df.at[x * NZ + z],
            drs.at[k], lambda x, z, y, c: drr.at[x * NZ + z], (0, dz, 0, 0),
        )
        for k, dz in enumerate(Z_NEAR)
    ]
    for item in forward:
        item.recv()
    if stop == 7:
        loads[6].wait()
        return finish()

    high, low = halves(pf[...].reshape(768, rank))
    pfh[...] = high
    pfl[...] = low
    me_q = x * NY + y

    def power_rows(start, size):
        own, near = gt[0, start : start + size, :], gt[1, start : start + size, :]
        return (mm(own, pfh[...]) + mm(near, pfh[...])) + (mm(own, pfl[...]) + mm(near, pfl[...]))

    def along_z(src, dst, ss, rs, dzs):
        return {
            dz: send(src((z + dz) % NZ), lambda x, z, y, c: dst(x, z, y), ss.at[k], lambda x, z, y, c: rs.at[z], (0, dz, 0, 0))
            for k, dz in enumerate(dzs)
        }

    def along_q(src, dst, ss, rs, pairs):
        return {
            (dx, dy): send(
                src(((x + dx) % NX) * NY + (y + dy) % NY), lambda x, z, y, c: dst(x, z, y),
                ss.at[k], lambda x, z, y, c: rs.at[x * NY + y], (dx, 0, dy, 0),
            )
            for k, (dx, dy) in enumerate(pairs)
        }

    pwb[...] = power_rows(512, 256).reshape(NZ, 32, rank)
    b_big = along_z(lambda n: pwb.at[n], lambda x, z, y: rb.at[z], bbs, bbr, Z_NEAR)
    pwa[...] = power_rows(0, 512).reshape(8, 64, rank)
    a_big = along_q(lambda n: pwa.at[n], lambda x, z, y: ra.at[x * NY + y], bas, bar_, Q_ALL)
    if stop == 8:
        loads[6].wait()
        return finish()

    part = pwb[z]
    for dz in Z_NEAR:
        b_big[dz].recv()
        part = part + rb[(z - dz + NZ) % NZ]
    for t in range(8):
        sb[t] = part[8 * (t // 2) : 8 * (t // 2) + 8, 128 * (t % 2) : 128 * (t % 2) + 128]
    b_small = along_q(lambda n: sb.at[n], lambda x, z, y: rb2.at[x * NY + y], sbs, sbr, Q_ALL)
    part = pwa[me_q]
    for dx, dy in Q_NEAR:
        a_big[dx, dy].recv()
        part = part + ra[((x + dx) % NX) * NY + (y - dy + NY) % NY]
    sa[...] = part.reshape(NZ, 8, rank)
    a_small = along_z(lambda n: sa.at[n], lambda x, z, y: ra2.at[z], sas, sar, Z_FAR)
    if stop == 9:
        loads[6].wait()
        return finish()

    for item in directions:
        item.recv()
    column = pl.ds(pl.multiple_of(x * NZ, NZ), NZ)
    dir_x = send(
        df.at[column], lambda x, z, y, c: df.at[pl.ds(pl.multiple_of(x * NZ, NZ), NZ)],
        drs.at[7], lambda *_: drr.at[16], XP,
    )

    part = sb[me_q]
    for dx, dy in Q_NEAR:
        b_small[dx, dy].recv()
        part = part + rb2[((x + dx) % NX) * NY + (y - dy + NY) % NY]
    zb[me_q] = part
    b_wide = along_q(lambda n: zb.at[me_q], lambda x, z, y: zb.at[x * NY + y], gbs, gbr, Q_ALL)
    part = sa[z]
    for dz in Z_NEAR:
        a_small[dz].recv()
        part = part + ra2[(z - dz + NZ) % NZ]
    fa[me_q, z] = part
    a_wide = along_z(lambda n: fa.at[me_q, z], lambda x, z, y: fa.at[x * NY + y, z], gas, gar, Z_FAR)
    if stop == 10:
        loads[6].wait()
        return finish()

    loads[6].wait()
    factor = learn_rate * galore_scale * scale

    def renew(j):
        column = (x + j) % NX
        rows = pl.ds(pl.multiple_of(384 * column, 384), 384)
        directed = halves(df[pl.ds(8 * column, 8)].reshape(384, rank))
        update = mm3(directed, (bt[0], bt[1]))
        wn[c, rows, :] = (w[rows, :].astype(f32) - factor * update).astype(bf16)
        send(
            wn.at[c, rows],
            lambda x, z, y, c: wn.at[c, pl.ds(pl.multiple_of(384 * ((x + j) % NX), 384), 384)],
            ws.at[j], lambda *_: wr.at[j], SIB,
        )

    renew(0)

    for item in b_wide.values():
        item.recv()
    for t in range(8):
        fb[z, 8 * (t // 2) : 8 * (t // 2) + 8, 128 * (t % 2) : 128 * (t % 2) + 128] = zb[t]
    b_full = along_z(lambda n: fb.at[z], lambda x, z, y: fb.at[z], hbs, hbr, Z_NEAR)
    for item in a_wide.values():
        item.recv()
    a_full = along_q(lambda n: fa.at[me_q], lambda x, z, y: fa.at[x * NY + y], has, har, Q_ALL)
    if stop == 11:
        return finish()

    dir_x.recv()
    renew(1)
    if stop == 12:
        return finish()

    for item in list(b_full.values()) + list(a_full.values()):
        item.recv()
    if stop == 13:
        return finish()

    power_a, power_b = fa[...].reshape(512, rank), fb[...].reshape(256, rank)
    norm = jnp.sqrt(jnp.sum(power_a * power_a) + jnp.sum(power_b * power_b))
    inverse = 1.0 / (norm + norm_eps)
    iterate = [power_b * inverse, power_a[:256] * inverse, power_a[256:] * inverse]
    split = [halves(item) for item in iterate]
    gram = None
    for high, low in split:
        term = mm3((high.T, low.T), (high, low))
        gram = term if gram is None else gram + term
    if stop == 14:
        bn[0, 0:256] = gram
        return finish()
    diagonal = (
        lax.broadcasted_iota(jnp.int32, (rank, rank), 0)
        == lax.broadcasted_iota(jnp.int32, (rank, rank), 1)
    )
    mix = None
    for sweep in range(NS_ITERS):
        gh = halves(gram)
        step = coeff_b * gram + coeff_c * mm3(gh, gh)
        step = step + jnp.where(diagonal, coeff_a, 0.0)
        sh = halves(step)
        mix = sh if mix is None else halves(mm3(mix, sh))
        if sweep < NS_ITERS - 1:
            gram = mm3(halves(mm3(gh, sh)), sh)
    if stop == 15:
        bn[0, 0:256] = mix[0].astype(f32)
        return finish()
    for k, start in enumerate((512, 0, 256)):
        rows = pl.ds(start, 256)
        bn[c, rows, :] = width**0.5 * mm3(split[k], mix)
        send(bn.at[c, rows], lambda x, z, y, c, rows=rows: bn.at[c, rows], bs.at[k], lambda *_, k=k: br.at[k], SIB)
    finish()


def write_out(wv, bv, v1, v2, wn, bn, o1, o2, sem):
    copies = [
        pltpu.make_async_copy(src, dst, sem.at[k])
        for k, (src, dst) in enumerate(((wv, wn), (bv, bn), (v1, o1), (v2, o2)))
    ]
    for item in copies:
        item.start()
    for item in copies:
        item.wait()


def body(grads, weights, basis, first, second):
    layers, width, rank = basis.shape
    any_spec = pl.BlockSpec(memory_space=pl.ANY)
    vmem_spec = pl.BlockSpec(memory_space=pltpu.VMEM)
    dma = pltpu.SemaphoreType.DMA
    results = ((weights.shape, bf16), (basis.shape, f32), (first.shape, f32), (second.shape, f32))
    held = pl.pallas_call(
        kernel,
        out_shape=tuple(pltpu.VMEM(shape, dtype) for shape, dtype in results),
        in_specs=[any_spec] * 5,
        out_specs=[vmem_spec] * 4,
        scratch_shapes=[
            pltpu.VMEM((2, 768, 768), bf16),
            pltpu.VMEM((768, 768), bf16),
            pltpu.VMEM((2, 768, 768), bf16),
            pltpu.VMEM((2, 768, 256), f32),
            pltpu.VMEM((2, 768, 256), bf16),
            pltpu.VMEM((2, 768, 256), bf16),
            pltpu.VMEM((2, 256, 768), bf16),
            pltpu.VMEM((768, 768), bf16),
            pltpu.VMEM((2, 16, 48, 256), f32),
            pltpu.VMEM((16, 48, 256), f32),
            pltpu.VMEM((8, 48, 256), f32),
            pltpu.VMEM((2, 8, 48, 256), f32),
            pltpu.VMEM((16, 48, 256), f32),
            pltpu.VMEM((768, 256), bf16),
            pltpu.VMEM((768, 256), bf16),
            pltpu.VMEM((16, 48, 256), f32),
            pltpu.VMEM((2, 2, 24, 256), f32),
            pltpu.VMEM((2, 2, 24, 256), f32),
            pltpu.VMEM((8, 64, 256), f32),
            pltpu.VMEM((8, 32, 256), f32),
            pltpu.VMEM((8, 64, 256), f32),
            pltpu.VMEM((8, 32, 256), f32),
            pltpu.VMEM((8, 8, 256), f32),
            pltpu.VMEM((8, 8, 128), f32),
            pltpu.VMEM((8, 8, 256), f32),
            pltpu.VMEM((8, 8, 128), f32),
            pltpu.VMEM((8, 8, 128), f32),
            pltpu.VMEM((8, 8, 8, 256), f32),
            pltpu.VMEM((8, 32, 256), f32),
            dma((7,)),
            dma((16,)), dma((16,)),
            dma((5,)), dma((5,)),
            dma((8,)), dma((8,)),
            dma((9,)), dma((2, 8)),
            dma((8,)), dma((16,)), dma((7,)),
            dma((8,)), dma((17,)),
            dma((7,)), dma((8,)),
            dma((7,)), dma((8,)),
            dma((7,)), dma((8,)),
            dma((7,)), dma((8,)),
            dma((7,)), dma((8,)),
            dma((7,)), dma((8,)),
            dma((7,)), dma((8,)),
            dma((7,)), dma((8,)),
            dma((2,)), dma((2,)),
            dma((3,)), dma((3,)),
        ],
        name="galore_step",
        compiler_params=pltpu.CompilerParams(
            collective_id=0, has_side_effects=True, vmem_limit_bytes=56 << 20
        ),
    )(grads, weights, basis, first, second)
    return pl.pallas_call(
        write_out,
        out_shape=tuple(jax.ShapeDtypeStruct(shape, dtype) for shape, dtype in results),
        in_specs=[vmem_spec] * 4,
        out_specs=[any_spec] * 4,
        scratch_shapes=[dma((4,))],
        name="write_out",
        compiler_params=pltpu.CompilerParams(vmem_limit_bytes=1 << 20),
    )(*(pltpu.with_memory_space_constraint(item, pltpu.VMEM) for item in held))


def solution(mesh):
    return jax.shard_map(
        body,
        mesh=mesh,
        in_specs=(
            P("shard", "section", "tensor", None),
            P("section", "tensor", None),
            P("section", None, None),
            P("section", ("tensor", "shard"), None),
            P("section", ("tensor", "shard"), None),
        ),
        out_specs=(
            P("section", "tensor", None),
            P("section", None, None),
            P("section", ("tensor", "shard"), None),
            P("section", ("tensor", "shard"), None),
        ),
        check_vma=False,
    )
```

```python
import jax
import jax.numpy as jnp
from jax import lax
from jax.experimental import pallas as pl
from jax.experimental.pallas import tpu as pltpu
from jax.sharding import PartitionSpec as P

NS_ITERS = 3
STEP = 1000

learn_rate = 0.5
galore_scale = 0.25
beta_one = 0.9
beta_two = 0.999
adam_eps = 1e-08
norm_eps = 1e-07
coeff_a = 3.4445
coeff_b = -4.775
coeff_c = 2.0315

f32 = jnp.float32
bf16 = jnp.bfloat16
MESH = pl.DeviceIdType.MESH

NX, NZ, NY = 2, 8, 4
Z_FAR = (4, 3, 5, 2, 6, 1, 7)
Z_NEAR = (1, 7, 2, 6, 3, 5, 4)
Q_NEAR = ((0, 1), (0, 3), (1, 0), (1, 1), (1, 3), (0, 2), (1, 2))
Q_SEND = ((1, 2), (1, 1), (1, 3), (1, 0), (0, 2), (0, 1), (0, 3))


def halves(value):
    high = value.astype(bf16)
    return high, (value - high.astype(f32)).astype(bf16)


def mm(a, b):
    return jnp.dot(a, b, preferred_element_type=f32)


def mm3(a, b):
    (ah, al), (bh, bl) = a, b
    return mm(ah, bh) + (mm(ah, bl) + mm(al, bh))


def adam(reduced, first, second):
    one = beta_one * first + (1.0 - beta_one) * reduced
    two = beta_two * second + (1.0 - beta_two) * reduced * reduced
    corrected_one = one / (1.0 - beta_one**STEP)
    corrected_two = two / (1.0 - beta_two**STEP)
    return one, two, corrected_one / (jnp.sqrt(corrected_two) + adam_eps)


class Flow:
    def __init__(self, me, log, src, dst, send, recv, rel):
        away = {
            "shard": (((me[0] + rel[0]) % NX) * NZ + (me[1] + rel[1]) % NZ) * 2 + (me[3] + rel[3]) % 2,
            "tensor": (me[2] + rel[2]) % NY,
        }
        sizes = (NX, NZ, NY, 2)
        back = tuple(m if r == 0 else (m - r + n) % n for m, r, n in zip(me, rel, sizes))
        self.out = pltpu.make_async_remote_copy(
            src_ref=src, dst_ref=dst(*me), send_sem=send, recv_sem=recv(*me), device_id=away, device_id_type=MESH
        )
        self.back = pltpu.make_async_remote_copy(
            src_ref=dst(*back), dst_ref=dst(*back), send_sem=send, recv_sem=recv(*back),
            device_id=away, device_id_type=MESH,
        )
        self.log = log
        self.waiting = True
        log.append(self)
        self.out.start()

    def recv(self):
        self.back.wait_recv()
        self.waiting = False

    def done(self):
        if self.waiting:
            self.recv()
        self.out.wait_send()


def dot(a, b, dims):
    return lax.dot_general(a, b, (dims, ((), ())), preferred_element_type=f32)


def kernel(
    grads, weights, basis, first, second,
    wn, bn, o1, o2,
    g, gs, b, bh, bl, w, p, ps, xr, rz, pf, phl, df, mo, mres, pw, r1, s2, r2, z2, pwf,
    lsem, sps, spr, ses, ser, xs, xrr, zs, zr, ags, agr, fws, drs, drr,
    p1s, p1r, p2s, p2r, q2s, q2r, q1s, q1r, ws, wr, bs, br,
    stop=99,
):
    s = lax.axis_index("shard")
    y = lax.axis_index("tensor")
    x, z, c = s // 16, (s // 2) % 8, s % 2
    me = (x, z, y, c)
    other = 1 - c
    ox = 1 - x
    width, rank = b.shape[1], b.shape[2]
    half = rank // 2
    scale = width ** (-0.5)
    mine = x * NZ + z
    me_q = x * NY + y
    log = []
    SIB, XP = (0, 0, 0, 1), (1, 0, 0, 0)
    HALVES = (0, 1)

    def send(src, dst, ss, rs, rel):
        return Flow(me, log, src, dst, ss, rs, rel)

    def finish():
        for item in log:
            item.done()

    barrier = pltpu.get_barrier_semaphore()
    peers = [SIB]
    peers += [(dx, 0, dy, 0) for dx in range(NX) for dy in range(NY) if (dx, dy) != (0, 0)]
    peers += [(0, dz, 0, 0) for dz in range(1, NZ)]
    for dx, dz, dy, dc in peers:
        dev = {"shard": (((x + dx) % NX) * NZ + (z + dz) % NZ) * 2 + (c + dc) % 2, "tensor": (y + dy) % NY}
        pl.semaphore_signal(barrier, 1, device_id=dev, device_id_type=MESH)

    loads = [
        pltpu.make_async_copy(basis.at[other], b.at[other], lsem.at[0]),
        pltpu.make_async_copy(grads.at[0, other], g.at[other], lsem.at[1]),
        pltpu.make_async_copy(basis.at[c], b.at[c], lsem.at[2]),
        pltpu.make_async_copy(grads.at[0, c], g.at[c], lsem.at[3]),
        pltpu.make_async_copy(first.at[c], mo.at[0, c], lsem.at[4]),
        pltpu.make_async_copy(second.at[c], mo.at[1, c], lsem.at[5]),
        pltpu.make_async_copy(weights.at[c], w, lsem.at[6]),
    ]
    for load in loads:
        load.start()

    def column_of(xx):
        return pl.ds(pl.multiple_of(xx * NZ, NZ), NZ)

    def project(layer, column):
        rows = pl.ds(pl.multiple_of(column * 384, 384), 384)
        left = g[layer, rows, :]
        out = mm(left, bh[layer]) + mm(left, bl[layer])
        for h in HALVES:
            p[h, layer, column_of(column)] = out[:, half * h : half * h + half].reshape(NZ, 48, half)

    def split_basis(layer):
        high, low = halves(b[layer])
        bh[layer] = high
        bl[layer] = low

    for k, layer in enumerate((other, c)):
        loads[2 * k].wait()
        split_basis(layer)
        loads[2 * k + 1].wait()
        project(layer, ox)
        project(layer, x)
    for load in loads[4:]:
        load.wait()
    pl.semaphore_wait(barrier, len(peers))

    to_sib = {}
    for h in HALVES:
        for dx in (1, 0):
            to_sib[h, dx] = send(
                p.at[h, other, column_of((x + dx) % NX)],
                lambda x, z, y, c: ps.at[h, column_of((x + dx) % NX)],
                sps.at[h, dx], lambda *_: spr.at[h, dx], SIB,
            )
    first_in = send(first.at[other], lambda x, z, y, c: mo.at[0, c], ses.at[1], lambda *_: ser.at[1], SIB)
    second_in = send(second.at[other], lambda x, z, y, c: mo.at[1, c], ses.at[2], lambda *_: ser.at[2], SIB)
    grads_in = send(g.at[other], lambda *_: gs, ses.at[0], lambda *_: ser.at[0], SIB)

    order = Z_FAR + (0,)

    def add_sib(h, dx):
        to_sib[h, dx].recv()
        rows = column_of((x + dx) % NX)
        p[h, c, rows] = p[h, c, rows] + ps[h, rows]

    over_x, over_z, gather, forward = {}, {}, {}, {}

    def exchange_x(h):
        add_sib(h, 1)
        for k, dz in enumerate(order):
            over_x[h, dz] = send(
                p.at[h, c, ox * NZ + (z + dz) % NZ],
                lambda x, z, y, c: xr.at[h, (z + dz) % NZ],
                xs.at[h, k], lambda *_: xrr.at[h, k], XP,
            )

    def scatter_z(h):
        add_sib(h, 0)
        for k, dz in enumerate(order):
            slot = (z + dz) % NZ
            n = x * NZ + slot
            over_x[h, dz].recv()
            if dz:
                p[h, c, n] = p[h, c, n] + xr[h, slot]
                over_z[h, dz] = send(
                    p.at[h, c, n], lambda x, z, y, c: rz.at[h, z], zs.at[h, k],
                    lambda x, z, y, c: zr.at[h, z], (0, dz, 0, 0),
                )
            else:
                rz[h, z] = p[h, c, n] + xr[h, slot]

    def gather_z(h):
        total = rz[h, z]
        for dz in Z_NEAR:
            over_z[h, dz].recv()
            total = total + rz[h, (z - dz + NZ) % NZ]
        pf[h, mine] = total
        for k, (dx, dz) in enumerate(((1, 0),) + tuple((0, dz) for dz in Z_NEAR)):
            gather[h, dz] = send(
                pf.at[h, mine], lambda x, z, y, c: pf.at[h, x * NZ + z], ags.at[h, k],
                lambda x, z, y, c: agr.at[h, x * NZ + z], (dx, dz, 0, 0),
            )
        return total

    def forward_x(h):
        for k, dz in enumerate(Z_NEAR):
            gather[h, dz].recv()
            forward[h, dz] = send(
                pf.at[h, x * NZ + (z - dz + NZ) % NZ],
                lambda x, z, y, c: pf.at[h, x * NZ + (z - dz + NZ) % NZ],
                fws.at[h, k],
                lambda x, z, y, c: agr.at[h, x * NZ + (z - dz + NZ) % NZ],
                XP,
            )

    exchange_x(0)
    exchange_x(1)
    scatter_z(0)
    if stop == 2:
        return finish()
    scatter_z(1)
    if stop == 3:
        return finish()
    totals = [gather_z(0)]
    if stop == 4:
        return finish()
    totals.append(gather_z(1))
    if stop == 5:
        return finish()

    first_in.recv()
    second_in.recv()
    one, two, direction = adam(
        scale * jnp.concatenate(totals, axis=1), mo[0].reshape(48, rank), mo[1].reshape(48, rank)
    )
    mres[0] = one.reshape(2, 24, rank)
    mres[1] = two.reshape(2, 24, rank)
    o1[c] = mres[0, c]
    o2[c] = mres[1, c]
    df[mine] = direction
    send(mres.at[0, other], lambda x, z, y, c: o1.at[c], ses.at[3], lambda *_: ser.at[3], SIB)
    send(mres.at[1, other], lambda x, z, y, c: o2.at[c], ses.at[4], lambda *_: ser.at[4], SIB)

    forward_x(0)
    forward_x(1)
    if stop == 6:
        return finish()
    dir_x = send(
        df.at[mine], lambda x, z, y, c: df.at[x * NZ + z], drs.at[14], lambda x, z, y, c: drr.at[x * NZ + z], XP
    )

    def send_directions(j):
        return [
            send(
                df.at[((x + j) % NX) * NZ + z],
                lambda x, z, y, c: df.at[((x + j) % NX) * NZ + z],
                drs.at[2 * k + j],
                lambda x, z, y, c: drr.at[((x + j) % NX) * NZ + z],
                (0, dz, 0, 0),
            )
            for k, dz in enumerate(Z_NEAR)
        ]

    def q_of(dx, dy):
        return ((x + dx) % NX) * NY + (y + dy) % NY

    over_q, over_z2, gather_z2, gather_q = {}, {}, {}, {}

    def power_part(h):
        gather[h, 0].recv()
        for dz in Z_NEAR:
            forward[h, dz].recv()
        high, low = halves(pf[h].reshape(768, half))
        phl[h, :, 0:half] = high
        phl[h, :, half:rank] = low
        right = phl[h]
        out = dot(g[c], right, ((0,), (0,))) + dot(gs[...], right, ((0,), (0,)))
        pw[h] = (out[:, 0:half] + out[:, half:rank]).reshape(8, 96, half)
        for k, (dx, dy) in enumerate(Q_SEND):
            over_q[h, dx, dy] = send(
                pw.at[h, q_of(dx, dy)], lambda x, z, y, c: r1.at[h, x * NY + y], p1s.at[h, k],
                lambda x, z, y, c: p1r.at[h, x * NY + y], (dx, 0, dy, 0),
            )

    def reduce_q(h):
        part = pw[h, me_q]
        for dx, dy in Q_NEAR:
            over_q[h, dx, dy].recv()
            part = part + r1[h, q_of(dx, NY - dy)]
        for t in range(NZ):
            s2[h, t, 0:12] = part[12 * t : 12 * t + 12]
        for k, dz in enumerate(Z_FAR):
            over_z2[h, dz] = send(
                s2.at[h, (z + dz) % NZ], lambda x, z, y, c: r2.at[h, z], p2s.at[h, k],
                lambda x, z, y, c: p2r.at[h, z], (0, dz, 0, 0),
            )

    def reduce_z(h):
        part = s2[h, z]
        for dz in Z_NEAR:
            over_z2[h, dz].recv()
            part = part + r2[h, (z - dz + NZ) % NZ]
        z2[h, z] = part
        for k, dz in enumerate(Z_FAR):
            gather_z2[h, dz] = send(
                z2.at[h, z], lambda x, z, y, c: z2.at[h, z], q2s.at[h, k],
                lambda x, z, y, c: q2r.at[h, z], (0, dz, 0, 0),
            )

    def spread_q(h):
        for dz in Z_NEAR:
            gather_z2[h, dz].recv()
        for t in range(NZ):
            pwf[h, me_q, 12 * t : 12 * t + 12] = z2[h, t, 0:12]
        for k, (dx, dy) in enumerate(Q_SEND):
            gather_q[h, dx, dy] = send(
                pwf.at[h, me_q], lambda x, z, y, c: pwf.at[h, x * NY + y], q1s.at[h, k],
                lambda x, z, y, c: q1r.at[h, x * NY + y], (dx, 0, dy, 0),
            )

    s2[...] = jnp.zeros_like(s2)
    grads_in.recv()
    power_part(0)
    if stop == 7:
        return finish()
    power_part(1)
    if stop == 8:
        return finish()
    directions = send_directions(0)
    reduce_q(0)
    if stop == 9:
        return finish()
    reduce_q(1)
    if stop == 10:
        return finish()
    reduce_z(0)
    reduce_z(1)
    if stop == 11:
        return finish()
    spread_q(0)
    spread_q(1)
    if stop == 12:
        return finish()
    dir_x.recv()
    others = send_directions(1)

    factor = learn_rate * galore_scale * scale

    def renew(j):
        column = (x + j) % NX
        rows = pl.ds(pl.multiple_of(384 * column, 384), 384)
        dh, dl = halves(df[column_of(column)].reshape(384, rank))
        across = ((1,), (1,))
        update = dot(dh, bh[c], across) + (dot(dh, bl[c], across) + dot(dl, bh[c], across))
        wn[c, rows, :] = (w[rows, :].astype(f32) - factor * update).astype(bf16)
        send(
            wn.at[c, rows],
            lambda x, z, y, c: wn.at[c, pl.ds(pl.multiple_of(384 * ((x + j) % NX), 384), 384)],
            ws.at[j], lambda *_: wr.at[j], SIB,
        )

    for item in directions:
        item.recv()
    renew(0)
    for item in others:
        item.recv()
    renew(1)
    if stop == 13:
        return finish()

    for item in gather_q.values():
        item.recv()
    if stop == 14:
        return finish()

    power = jnp.concatenate([pwf[h].reshape(768, half) for h in HALVES], axis=1)
    norm = jnp.sqrt(jnp.sum(power * power))
    iterate = power * (1.0 / (norm + norm_eps))
    it = halves(iterate)
    gram = mm3((it[0].T, it[1].T), it)
    diagonal = (
        lax.broadcasted_iota(jnp.int32, (rank, rank), 0)
        == lax.broadcasted_iota(jnp.int32, (rank, rank), 1)
    )
    mix = None
    for sweep in range(NS_ITERS):
        gh = halves(gram)
        step = coeff_b * gram + coeff_c * mm3(gh, gh)
        step = step + jnp.where(diagonal, coeff_a, 0.0)
        sh = halves(step)
        mix = sh if mix is None else halves(mm3(mix, sh))
        if sweep < NS_ITERS - 1:
            gram = mm3(halves(mm3(gh, sh)), sh)
    for k in range(2):
        rows = pl.ds(384 * k, 384)
        left = halves(iterate[384 * k : 384 * k + 384])
        bn[c, rows, :] = width**0.5 * mm3(left, mix)
        send(bn.at[c, rows], lambda x, z, y, c, rows=rows: bn.at[c, rows], bs.at[k], lambda *_, k=k: br.at[k], SIB)
    finish()


def write_out(wv, bv, v1, v2, wn, bn, o1, o2, sem):
    pairs = [(v1, o1), (v2, o2)]
    pairs += [(wv.at[k // 2, pl.ds(384 * (k % 2), 384)], wn.at[k // 2, pl.ds(384 * (k % 2), 384)]) for k in range(4)]
    pairs += [(bv.at[k], bn.at[k]) for k in range(2)]
    copies = [pltpu.make_async_copy(src, dst, sem.at[k]) for k, (src, dst) in enumerate(pairs)]
    for item in copies:
        item.start()
    for item in copies:
        item.wait()


def body(grads, weights, basis, first, second):
    layers, width, rank = basis.shape
    any_spec = pl.BlockSpec(memory_space=pl.ANY)
    vmem_spec = pl.BlockSpec(memory_space=pltpu.VMEM)
    dma = pltpu.SemaphoreType.DMA
    results = ((weights.shape, bf16), (basis.shape, f32), (first.shape, f32), (second.shape, f32))
    held = pl.pallas_call(
        kernel,
        out_shape=tuple(pltpu.VMEM(shape, dtype) for shape, dtype in results),
        in_specs=[any_spec] * 5,
        out_specs=[vmem_spec] * 4,
        scratch_shapes=[
            pltpu.VMEM((2, 768, 768), bf16),
            pltpu.VMEM((768, 768), bf16),
            pltpu.VMEM((2, 768, 256), f32),
            pltpu.VMEM((2, 768, 256), bf16),
            pltpu.VMEM((2, 768, 256), bf16),
            pltpu.VMEM((768, 768), bf16),
            pltpu.VMEM((2, 2, 16, 48, 128), f32),
            pltpu.VMEM((2, 16, 48, 128), f32),
            pltpu.VMEM((2, 8, 48, 128), f32),
            pltpu.VMEM((2, 8, 48, 128), f32),
            pltpu.VMEM((2, 16, 48, 128), f32),
            pltpu.VMEM((2, 768, 256), bf16),
            pltpu.VMEM((16, 48, 256), f32),
            pltpu.VMEM((2, 2, 24, 256), f32),
            pltpu.VMEM((2, 2, 24, 256), f32),
            pltpu.VMEM((2, 8, 96, 128), f32),
            pltpu.VMEM((2, 8, 96, 128), f32),
            pltpu.VMEM((2, 8, 16, 128), f32),
            pltpu.VMEM((2, 8, 16, 128), f32),
            pltpu.VMEM((2, 8, 16, 128), f32),
            pltpu.VMEM((2, 8, 96, 128), f32),
            dma((7,)),
            dma((2, 2)), dma((2, 2)),
            dma((5,)), dma((5,)),
            dma((2, 8)), dma((2, 8)),
            dma((2, 8)), dma((2, 8)),
            dma((2, 8)), dma((2, 16)), dma((2, 7)),
            dma((15,)), dma((16,)),
            dma((2, 7)), dma((2, 8)),
            dma((2, 7)), dma((2, 8)),
            dma((2, 7)), dma((2, 8)),
            dma((2, 7)), dma((2, 8)),
            dma((2,)), dma((2,)),
            dma((2,)), dma((2,)),
        ],
        name="galore_step",
        compiler_params=pltpu.CompilerParams(
            collective_id=0, has_side_effects=True, vmem_limit_bytes=56 << 20
        ),
    )(grads, weights, basis, first, second)
    return pl.pallas_call(
        write_out,
        out_shape=tuple(jax.ShapeDtypeStruct(shape, dtype) for shape, dtype in results),
        in_specs=[vmem_spec] * 4,
        out_specs=[any_spec] * 4,
        scratch_shapes=[dma((8,))],
        name="write_out",
        compiler_params=pltpu.CompilerParams(vmem_limit_bytes=1 << 20),
    )(*(pltpu.with_memory_space_constraint(item, pltpu.VMEM) for item in held))


def solution(mesh):
    return jax.shard_map(
        body,
        mesh=mesh,
        in_specs=(
            P("shard", "section", "tensor", None),
            P("section", "tensor", None),
            P("section", None, None),
            P("section", ("tensor", "shard"), None),
            P("section", ("tensor", "shard"), None),
        ),
        out_specs=(
            P("section", "tensor", None),
            P("section", None, None),
            P("section", ("tensor", "shard"), None),
            P("section", ("tensor", "shard"), None),
        ),
        check_vma=False,
    )
```

```python
import jax
import jax.numpy as jnp
from jax import lax
from jax.experimental import pallas as pl
from jax.experimental.pallas import tpu as pltpu
from jax.sharding import PartitionSpec as P

NS_ITERS = 3
STEP = 1000

learn_rate = 0.5
galore_scale = 0.25
beta_one = 0.9
beta_two = 0.999
adam_eps = 1e-08
norm_eps = 1e-07
coeff_a = 3.4445
coeff_b = -4.775
coeff_c = 2.0315

f32 = jnp.float32
bf16 = jnp.bfloat16
MESH = pl.DeviceIdType.MESH

NX, NZ, NY = 2, 8, 4
Z_FAR = (4, 3, 5, 2, 6, 1, 7)
Z_NEAR = (1, 7, 2, 6, 3, 5, 4)
Q_NEAR = ((0, 1), (0, 3), (1, 0), (1, 1), (1, 3), (0, 2), (1, 2))
Q_SEND = ((1, 2), (1, 1), (1, 3), (1, 0), (0, 2), (0, 1), (0, 3))


def halves(value):
    high = value.astype(bf16)
    return high, (value - high.astype(f32)).astype(bf16)


def mm(a, b):
    return jnp.dot(a, b, preferred_element_type=f32)


def mm3(a, b):
    (ah, al), (bh, bl) = a, b
    return mm(ah, bh) + (mm(ah, bl) + mm(al, bh))


def adam(reduced, first, second):
    one = beta_one * first + (1.0 - beta_one) * reduced
    two = beta_two * second + (1.0 - beta_two) * reduced * reduced
    corrected_one = one / (1.0 - beta_one**STEP)
    corrected_two = two / (1.0 - beta_two**STEP)
    return one, two, corrected_one / (jnp.sqrt(corrected_two) + adam_eps)


class Flow:
    def __init__(self, me, log, src, dst, send, recv, rel):
        away = {
            "shard": (((me[0] + rel[0]) % NX) * NZ + (me[1] + rel[1]) % NZ) * 2 + (me[3] + rel[3]) % 2,
            "tensor": (me[2] + rel[2]) % NY,
        }
        sizes = (NX, NZ, NY, 2)
        back = tuple(m if r == 0 else (m - r + n) % n for m, r, n in zip(me, rel, sizes))
        self.out = pltpu.make_async_remote_copy(
            src_ref=src, dst_ref=dst(*me), send_sem=send, recv_sem=recv(*me), device_id=away, device_id_type=MESH
        )
        self.back = pltpu.make_async_remote_copy(
            src_ref=dst(*back), dst_ref=dst(*back), send_sem=send, recv_sem=recv(*back),
            device_id=away, device_id_type=MESH,
        )
        self.log = log
        self.waiting = True
        log.append(self)
        self.out.start()

    def recv(self):
        self.back.wait_recv()
        self.waiting = False

    def done(self):
        if self.waiting:
            self.recv()
        self.out.wait_send()


def dot(a, b, dims):
    return lax.dot_general(a, b, (dims, ((), ())), preferred_element_type=f32)


def kernel(
    grads, weights, basis, first, second,
    wn, bn, o1, o2,
    g, gs, b, bh, bl, w, p, ps, xr, rz, pf, phl, df, mo, mres, pw, r1, s2, r2, z2, pwf,
    lsem, sps, spr, ses, ser, xs, xrr, zs, zr, ags, agr, fws, drs, drr,
    p1s, p1r, p2s, p2r, q2s, q2r, q1s, q1r, ws, wr, bs, br,
    stop=99,
):
    s = lax.axis_index("shard")
    y = lax.axis_index("tensor")
    x, z, c = s // 16, (s // 2) % 8, s % 2
    me = (x, z, y, c)
    other = 1 - c
    ox = 1 - x
    width, rank = b.shape[1], b.shape[2]
    half = rank // 2
    scale = width ** (-0.5)
    mine = x * NZ + z
    me_q = x * NY + y
    log = []
    SIB, XP = (0, 0, 0, 1), (1, 0, 0, 0)
    HALVES = (0, 1)

    def send(src, dst, ss, rs, rel):
        return Flow(me, log, src, dst, ss, rs, rel)

    def finish():
        for item in log:
            item.done()

    barrier = pltpu.get_barrier_semaphore()
    peers = [SIB]
    peers += [(dx, 0, dy, 0) for dx in range(NX) for dy in range(NY) if (dx, dy) != (0, 0)]
    peers += [(0, dz, 0, 0) for dz in range(1, NZ)]
    for dx, dz, dy, dc in peers:
        dev = {"shard": (((x + dx) % NX) * NZ + (z + dz) % NZ) * 2 + (c + dc) % 2, "tensor": (y + dy) % NY}
        pl.semaphore_signal(barrier, 1, device_id=dev, device_id_type=MESH)

    loads = [
        pltpu.make_async_copy(basis.at[other], b.at[other], lsem.at[0]),
        pltpu.make_async_copy(grads.at[0, other], g.at[other], lsem.at[1]),
        pltpu.make_async_copy(basis.at[c], b.at[c], lsem.at[2]),
        pltpu.make_async_copy(grads.at[0, c], g.at[c], lsem.at[3]),
        pltpu.make_async_copy(first.at[c], mo.at[0, c], lsem.at[4]),
        pltpu.make_async_copy(second.at[c], mo.at[1, c], lsem.at[5]),
        pltpu.make_async_copy(weights.at[c], w, lsem.at[6]),
    ]
    for load in loads:
        load.start()

    def column_of(xx):
        return pl.ds(pl.multiple_of(xx * NZ, NZ), NZ)

    def project(layer, column):
        rows = pl.ds(pl.multiple_of(column * 384, 384), 384)
        left = g[layer, rows, :]
        out = mm(left, bh[layer]) + mm(left, bl[layer])
        for h in HALVES:
            p[h, layer, column_of(column)] = out[:, half * h : half * h + half].reshape(NZ, 48, half)

    def split_basis(layer):
        high, low = halves(b[layer])
        bh[layer] = high
        bl[layer] = low

    for k, layer in enumerate((other, c)):
        loads[2 * k].wait()
        split_basis(layer)
        loads[2 * k + 1].wait()
        project(layer, ox)
        project(layer, x)
    for load in loads[4:]:
        load.wait()
    pl.semaphore_wait(barrier, len(peers))

    to_sib = {}
    for h in HALVES:
        for dx in (1, 0):
            to_sib[h, dx] = send(
                p.at[h, other, column_of((x + dx) % NX)],
                lambda x, z, y, c: ps.at[h, column_of((x + dx) % NX)],
                sps.at[h, dx], lambda *_: spr.at[h, dx], SIB,
            )
    first_in = send(first.at[other], lambda x, z, y, c: mo.at[0, c], ses.at[1], lambda *_: ser.at[1], SIB)
    second_in = send(second.at[other], lambda x, z, y, c: mo.at[1, c], ses.at[2], lambda *_: ser.at[2], SIB)

    order = Z_FAR + (0,)

    def add_sib(h, dx):
        to_sib[h, dx].recv()
        rows = column_of((x + dx) % NX)
        p[h, c, rows] = p[h, c, rows] + ps[h, rows]

    over_x, over_z, gather, forward = {}, {}, {}, {}

    def exchange_x(h):
        add_sib(h, 1)
        for k, dz in enumerate(order):
            over_x[h, dz] = send(
                p.at[h, c, ox * NZ + (z + dz) % NZ],
                lambda x, z, y, c: xr.at[h, (z + dz) % NZ],
                xs.at[h, k], lambda *_: xrr.at[h, k], XP,
            )

    def scatter_z(h):
        add_sib(h, 0)
        for k, dz in enumerate(order):
            slot = (z + dz) % NZ
            n = x * NZ + slot
            over_x[h, dz].recv()
            if dz:
                p[h, c, n] = p[h, c, n] + xr[h, slot]
                over_z[h, dz] = send(
                    p.at[h, c, n], lambda x, z, y, c: rz.at[h, z], zs.at[h, k],
                    lambda x, z, y, c: zr.at[h, z], (0, dz, 0, 0),
                )
            else:
                rz[h, z] = p[h, c, n] + xr[h, slot]

    def gather_z(h):
        total = rz[h, z]
        for dz in Z_NEAR:
            over_z[h, dz].recv()
            total = total + rz[h, (z - dz + NZ) % NZ]
        pf[h, mine] = total
        for k, (dx, dz) in enumerate(((1, 0),) + tuple((0, dz) for dz in Z_NEAR)):
            gather[h, dz] = send(
                pf.at[h, mine], lambda x, z, y, c: pf.at[h, x * NZ + z], ags.at[h, k],
                lambda x, z, y, c: agr.at[h, x * NZ + z], (dx, dz, 0, 0),
            )
        return total

    def forward_x(h):
        for k, dz in enumerate(Z_NEAR):
            gather[h, dz].recv()
            forward[h, dz] = send(
                pf.at[h, x * NZ + (z - dz + NZ) % NZ],
                lambda x, z, y, c: pf.at[h, x * NZ + (z - dz + NZ) % NZ],
                fws.at[h, k],
                lambda x, z, y, c: agr.at[h, x * NZ + (z - dz + NZ) % NZ],
                XP,
            )

    exchange_x(0)
    exchange_x(1)
    grads_in = send(g.at[other], lambda *_: gs, ses.at[0], lambda *_: ser.at[0], SIB)
    scatter_z(0)
    if stop == 2:
        return finish()
    scatter_z(1)
    if stop == 3:
        return finish()
    totals = [gather_z(0)]
    if stop == 4:
        return finish()
    totals.append(gather_z(1))
    if stop == 5:
        return finish()

    first_in.recv()
    second_in.recv()
    one, two, direction = adam(
        scale * jnp.concatenate(totals, axis=1), mo[0].reshape(48, rank), mo[1].reshape(48, rank)
    )
    mres[0] = one.reshape(2, 24, rank)
    mres[1] = two.reshape(2, 24, rank)
    o1[c] = mres[0, c]
    o2[c] = mres[1, c]
    df[mine] = direction
    send(mres.at[0, other], lambda x, z, y, c: o1.at[c], ses.at[3], lambda *_: ser.at[3], SIB)
    send(mres.at[1, other], lambda x, z, y, c: o2.at[c], ses.at[4], lambda *_: ser.at[4], SIB)

    forward_x(0)
    forward_x(1)
    if stop == 6:
        return finish()
    directions = [
        send(
            df.at[mine], lambda x, z, y, c: df.at[x * NZ + z], drs.at[k],
            lambda x, z, y, c: drr.at[z], (0, dz, 0, 0),
        )
        for k, dz in enumerate(Z_NEAR)
    ]

    def q_of(dx, dy):
        return ((x + dx) % NX) * NY + (y + dy) % NY

    over_q, over_z2, gather_z2, gather_q = {}, {}, {}, {}

    def power_part(h):
        gather[h, 0].recv()
        for dz in Z_NEAR:
            forward[h, dz].recv()
        high, low = halves(pf[h].reshape(768, half))
        phl[h, :, 0:half] = high
        phl[h, :, half:rank] = low
        right = phl[h]
        out = dot(g[c], right, ((0,), (0,))) + dot(gs[...], right, ((0,), (0,)))
        pw[h] = (out[:, 0:half] + out[:, half:rank]).reshape(8, 96, half)
        for k, (dx, dy) in enumerate(Q_SEND):
            over_q[h, dx, dy] = send(
                pw.at[h, q_of(dx, dy)], lambda x, z, y, c: r1.at[h, x * NY + y], p1s.at[h, k],
                lambda x, z, y, c: p1r.at[h, x * NY + y], (dx, 0, dy, 0),
            )

    def reduce_q(h):
        part = pw[h, me_q]
        for dx, dy in Q_NEAR:
            over_q[h, dx, dy].recv()
            part = part + r1[h, q_of(dx, NY - dy)]
        for t in range(NZ):
            s2[h, t, 0:12] = part[12 * t : 12 * t + 12]
        for k, dz in enumerate(Z_FAR):
            over_z2[h, dz] = send(
                s2.at[h, (z + dz) % NZ], lambda x, z, y, c: r2.at[h, z], p2s.at[h, k],
                lambda x, z, y, c: p2r.at[h, z], (0, dz, 0, 0),
            )

    def reduce_z(h):
        part = s2[h, z]
        for dz in Z_NEAR:
            over_z2[h, dz].recv()
            part = part + r2[h, (z - dz + NZ) % NZ]
        z2[h, z] = part
        for k, dz in enumerate(Z_FAR):
            gather_z2[h, dz] = send(
                z2.at[h, z], lambda x, z, y, c: z2.at[h, z], q2s.at[h, k],
                lambda x, z, y, c: q2r.at[h, z], (0, dz, 0, 0),
            )

    def spread_q(h):
        for dz in Z_NEAR:
            gather_z2[h, dz].recv()
        for t in range(NZ):
            pwf[h, me_q, 12 * t : 12 * t + 12] = z2[h, t, 0:12]
        for k, (dx, dy) in enumerate(Q_SEND):
            gather_q[h, dx, dy] = send(
                pwf.at[h, me_q], lambda x, z, y, c: pwf.at[h, x * NY + y], q1s.at[h, k],
                lambda x, z, y, c: q1r.at[h, x * NY + y], (dx, 0, dy, 0),
            )

    s2[...] = jnp.zeros_like(s2)
    grads_in.recv()
    power_part(0)
    if stop == 7:
        return finish()
    power_part(1)
    if stop == 8:
        return finish()
    reduce_q(0)
    if stop == 9:
        return finish()
    reduce_q(1)
    if stop == 10:
        return finish()
    for item in directions:
        item.recv()
    dir_x = send(
        df.at[column_of(x)], lambda x, z, y, c: df.at[column_of(x)], drs.at[7], lambda *_: drr.at[8], XP
    )
    factor = learn_rate * galore_scale * scale

    def renew(j):
        column = (x + j) % NX
        rows = pl.ds(pl.multiple_of(384 * column, 384), 384)
        dh, dl = halves(df[column_of(column)].reshape(384, rank))
        across = ((1,), (1,))
        update = dot(dh, bh[c], across) + (dot(dh, bl[c], across) + dot(dl, bh[c], across))
        wn[c, rows, :] = (w[rows, :].astype(f32) - factor * update).astype(bf16)
        send(
            wn.at[c, rows],
            lambda x, z, y, c: wn.at[c, pl.ds(pl.multiple_of(384 * ((x + j) % NX), 384), 384)],
            ws.at[j], lambda *_: wr.at[j], SIB,
        )

    reduce_z(0)
    reduce_z(1)
    if stop == 11:
        return finish()
    renew(0)
    spread_q(0)
    spread_q(1)
    if stop == 12:
        return finish()
    dir_x.recv()
    renew(1)
    if stop == 13:
        return finish()

    for item in gather_q.values():
        item.recv()
    if stop == 14:
        return finish()

    power = jnp.concatenate([pwf[h].reshape(768, half) for h in HALVES], axis=1)
    norm = jnp.sqrt(jnp.sum(power * power))
    iterate = power * (1.0 / (norm + norm_eps))
    it = halves(iterate)
    gram = mm3((it[0].T, it[1].T), it)
    diagonal = (
        lax.broadcasted_iota(jnp.int32, (rank, rank), 0)
        == lax.broadcasted_iota(jnp.int32, (rank, rank), 1)
    )
    mix = None
    for sweep in range(NS_ITERS):
        gh = halves(gram)
        step = coeff_b * gram + coeff_c * mm3(gh, gh)
        step = step + jnp.where(diagonal, coeff_a, 0.0)
        sh = halves(step)
        mix = sh if mix is None else halves(mm3(mix, sh))
        if sweep < NS_ITERS - 1:
            gram = mm3(halves(mm3(gh, sh)), sh)
    for k in range(2):
        rows = pl.ds(384 * k, 384)
        left = halves(iterate[384 * k : 384 * k + 384])
        bn[c, rows, :] = width**0.5 * mm3(left, mix)
        send(bn.at[c, rows], lambda x, z, y, c, rows=rows: bn.at[c, rows], bs.at[k], lambda *_, k=k: br.at[k], SIB)
    finish()


def write_out(wv, bv, v1, v2, wn, bn, o1, o2, sem):
    pairs = [(v1, o1), (v2, o2)]
    pairs += [(wv.at[k // 2, pl.ds(384 * (k % 2), 384)], wn.at[k // 2, pl.ds(384 * (k % 2), 384)]) for k in range(4)]
    pairs += [(bv.at[k], bn.at[k]) for k in range(2)]
    copies = [pltpu.make_async_copy(src, dst, sem.at[k]) for k, (src, dst) in enumerate(pairs)]
    for item in copies:
        item.start()
    for item in copies:
        item.wait()


def body(grads, weights, basis, first, second):
    layers, width, rank = basis.shape
    any_spec = pl.BlockSpec(memory_space=pl.ANY)
    vmem_spec = pl.BlockSpec(memory_space=pltpu.VMEM)
    dma = pltpu.SemaphoreType.DMA
    results = ((weights.shape, bf16), (basis.shape, f32), (first.shape, f32), (second.shape, f32))
    held = pl.pallas_call(
        kernel,
        out_shape=tuple(pltpu.VMEM(shape, dtype) for shape, dtype in results),
        in_specs=[any_spec] * 5,
        out_specs=[vmem_spec] * 4,
        scratch_shapes=[
            pltpu.VMEM((2, 768, 768), bf16),
            pltpu.VMEM((768, 768), bf16),
            pltpu.VMEM((2, 768, 256), f32),
            pltpu.VMEM((2, 768, 256), bf16),
            pltpu.VMEM((2, 768, 256), bf16),
            pltpu.VMEM((768, 768), bf16),
            pltpu.VMEM((2, 2, 16, 48, 128), f32),
            pltpu.VMEM((2, 16, 48, 128), f32),
            pltpu.VMEM((2, 8, 48, 128), f32),
            pltpu.VMEM((2, 8, 48, 128), f32),
            pltpu.VMEM((2, 16, 48, 128), f32),
            pltpu.VMEM((2, 768, 256), bf16),
            pltpu.VMEM((16, 48, 256), f32),
            pltpu.VMEM((2, 2, 24, 256), f32),
            pltpu.VMEM((2, 2, 24, 256), f32),
            pltpu.VMEM((2, 8, 96, 128), f32),
            pltpu.VMEM((2, 8, 96, 128), f32),
            pltpu.VMEM((2, 8, 16, 128), f32),
            pltpu.VMEM((2, 8, 16, 128), f32),
            pltpu.VMEM((2, 8, 16, 128), f32),
            pltpu.VMEM((2, 8, 96, 128), f32),
            dma((7,)),
            dma((2, 2)), dma((2, 2)),
            dma((5,)), dma((5,)),
            dma((2, 8)), dma((2, 8)),
            dma((2, 8)), dma((2, 8)),
            dma((2, 8)), dma((2, 16)), dma((2, 7)),
            dma((8,)), dma((9,)),
            dma((2, 7)), dma((2, 8)),
            dma((2, 7)), dma((2, 8)),
            dma((2, 7)), dma((2, 8)),
            dma((2, 7)), dma((2, 8)),
            dma((2,)), dma((2,)),
            dma((2,)), dma((2,)),
        ],
        name="galore_step",
        compiler_params=pltpu.CompilerParams(
            collective_id=0, has_side_effects=True, vmem_limit_bytes=56 << 20
        ),
    )(grads, weights, basis, first, second)
    return pl.pallas_call(
        write_out,
        out_shape=tuple(jax.ShapeDtypeStruct(shape, dtype) for shape, dtype in results),
        in_specs=[vmem_spec] * 4,
        out_specs=[any_spec] * 4,
        scratch_shapes=[dma((8,))],
        name="write_out",
        compiler_params=pltpu.CompilerParams(vmem_limit_bytes=1 << 20),
    )(*(pltpu.with_memory_space_constraint(item, pltpu.VMEM) for item in held))


def solution(mesh):
    return jax.shard_map(
        body,
        mesh=mesh,
        in_specs=(
            P("shard", "section", "tensor", None),
            P("section", "tensor", None),
            P("section", None, None),
            P("section", ("tensor", "shard"), None),
            P("section", ("tensor", "shard"), None),
        ),
        out_specs=(
            P("section", "tensor", None),
            P("section", None, None),
            P("section", ("tensor", "shard"), None),
            P("section", ("tensor", "shard"), None),
        ),
        check_vma=False,
    )
```

```python
import jax
import jax.numpy as jnp
from jax import lax
from jax.experimental import pallas as pl
from jax.experimental.pallas import tpu as pltpu
from jax.sharding import PartitionSpec as P

NS_ITERS = 3
STEP = 1000

learn_rate = 0.5
galore_scale = 0.25
beta_one = 0.9
beta_two = 0.999
adam_eps = 1e-08
norm_eps = 1e-07
coeff_a = 3.4445
coeff_b = -4.775
coeff_c = 2.0315

f32 = jnp.float32
bf16 = jnp.bfloat16
MESH = pl.DeviceIdType.MESH

NX, NZ, NY = 2, 8, 4
Z_FAR = (4, 3, 5, 2, 6, 1, 7)
Z_NEAR = (1, 7, 2, 6, 3, 5, 4)
Q_NEAR = ((0, 1), (0, 3), (1, 0), (1, 1), (1, 3), (0, 2), (1, 2))
Q_SEND = ((1, 2), (1, 1), (1, 3), (1, 0), (0, 2), (0, 1), (0, 3))


def halves(value):
    high = value.astype(bf16)
    return high, (value - high.astype(f32)).astype(bf16)


def mm(a, b):
    return jnp.dot(a, b, preferred_element_type=f32)


def mm3(a, b):
    (ah, al), (bh, bl) = a, b
    return mm(ah, bh) + (mm(ah, bl) + mm(al, bh))


def adam(reduced, first, second):
    one = beta_one * first + (1.0 - beta_one) * reduced
    two = beta_two * second + (1.0 - beta_two) * reduced * reduced
    corrected_one = one / (1.0 - beta_one**STEP)
    corrected_two = two / (1.0 - beta_two**STEP)
    return one, two, corrected_one / (jnp.sqrt(corrected_two) + adam_eps)


class Flow:
    def __init__(self, me, log, src, dst, send, recv, rel):
        away = {
            "shard": (((me[0] + rel[0]) % NX) * NZ + (me[1] + rel[1]) % NZ) * 2 + (me[3] + rel[3]) % 2,
            "tensor": (me[2] + rel[2]) % NY,
        }
        sizes = (NX, NZ, NY, 2)
        back = tuple(m if r == 0 else (m - r + n) % n for m, r, n in zip(me, rel, sizes))
        self.out = pltpu.make_async_remote_copy(
            src_ref=src, dst_ref=dst(*me), send_sem=send, recv_sem=recv(*me), device_id=away, device_id_type=MESH
        )
        self.back = pltpu.make_async_remote_copy(
            src_ref=dst(*back), dst_ref=dst(*back), send_sem=send, recv_sem=recv(*back),
            device_id=away, device_id_type=MESH,
        )
        self.log = log
        self.waiting = True
        log.append(self)
        self.out.start()

    def recv(self):
        self.back.wait_recv()
        self.waiting = False

    def done(self):
        if self.waiting:
            self.recv()
        self.out.wait_send()


def dot(a, b, dims):
    return lax.dot_general(a, b, (dims, ((), ())), preferred_element_type=f32)


def kernel(
    grads, weights, basis, first, second,
    wn, bn, o1, o2,
    g, gs, b, bh, bl, w, p, ps, xr, rz, pf, phl, df, mo, mres, pw, r1, s2, r2, z2, pwf,
    lsem, sps, spr, ses, ser, xs, xrr, zs, zr, ags, agr, fws, drs, drr,
    p1s, p1r, p2s, p2r, q2s, q2r, q1s, q1r, ws, wr, bs, br,
):
    s = lax.axis_index("shard")
    y = lax.axis_index("tensor")
    x, z, c = s // 16, (s // 2) % 8, s % 2
    me = (x, z, y, c)
    other = 1 - c
    ox = 1 - x
    width, rank = b.shape[1], b.shape[2]
    half = rank // 2
    scale = width ** (-0.5)
    mine = x * NZ + z
    me_q = x * NY + y
    log = []
    SIB, XP = (0, 0, 0, 1), (1, 0, 0, 0)
    HALVES = (0, 1)

    def send(src, dst, ss, rs, rel):
        return Flow(me, log, src, dst, ss, rs, rel)

    def settle(count):
        for item in log[:count]:
            item.done()
        del log[:count]

    def finish():
        settle(len(log))

    barrier = pltpu.get_barrier_semaphore()
    peers = [SIB]
    peers += [(dx, 0, dy, 0) for dx in range(NX) for dy in range(NY) if (dx, dy) != (0, 0)]
    peers += [(0, dz, 0, 0) for dz in range(1, NZ)]
    for dx, dz, dy, dc in peers:
        dev = {"shard": (((x + dx) % NX) * NZ + (z + dz) % NZ) * 2 + (c + dc) % 2, "tensor": (y + dy) % NY}
        pl.semaphore_signal(barrier, 1, device_id=dev, device_id_type=MESH)

    loads = [
        pltpu.make_async_copy(basis.at[other], b.at[other], lsem.at[0]),
        pltpu.make_async_copy(grads.at[0, other], g.at[other], lsem.at[1]),
        pltpu.make_async_copy(basis.at[c], b.at[c], lsem.at[2]),
        pltpu.make_async_copy(grads.at[0, c], g.at[c], lsem.at[3]),
        pltpu.make_async_copy(first.at[c], mo.at[0, c], lsem.at[4]),
        pltpu.make_async_copy(second.at[c], mo.at[1, c], lsem.at[5]),
        pltpu.make_async_copy(weights.at[c], w, lsem.at[6]),
    ]
    for load in loads:
        load.start()

    def column_of(xx):
        return pl.ds(pl.multiple_of(xx * NZ, NZ), NZ)

    def project(layer, column):
        rows = pl.ds(pl.multiple_of(column * 384, 384), 384)
        left = g[layer, rows, :]
        out = mm(left, bh[layer]) + mm(left, bl[layer])
        for h in HALVES:
            p[h, layer, column_of(column)] = out[:, half * h : half * h + half].reshape(NZ, 48, half)

    def split_basis(layer):
        high, low = halves(b[layer])
        bh[layer] = high
        bl[layer] = low

    for k, layer in enumerate((other, c)):
        loads[2 * k].wait()
        split_basis(layer)
        loads[2 * k + 1].wait()
        project(layer, ox)
        project(layer, x)
    for load in loads[4:]:
        load.wait()
    pl.semaphore_wait(barrier, len(peers))

    to_sib = {}
    for h in HALVES:
        for dx in (1, 0):
            to_sib[h, dx] = send(
                p.at[h, other, column_of((x + dx) % NX)],
                lambda x, z, y, c: ps.at[h, column_of((x + dx) % NX)],
                sps.at[h, dx], lambda *_: spr.at[h, dx], SIB,
            )
    first_in = send(first.at[other], lambda x, z, y, c: mo.at[0, c], ses.at[1], lambda *_: ser.at[1], SIB)
    second_in = send(second.at[other], lambda x, z, y, c: mo.at[1, c], ses.at[2], lambda *_: ser.at[2], SIB)

    order = Z_FAR + (0,)

    def add_sib(h, dx):
        to_sib[h, dx].recv()
        rows = column_of((x + dx) % NX)
        p[h, c, rows] = p[h, c, rows] + ps[h, rows]

    over_x, over_z, gather, forward = {}, {}, {}, {}

    def exchange_x(h):
        add_sib(h, 1)
        for k, dz in enumerate(order):
            over_x[h, dz] = send(
                p.at[h, c, ox * NZ + (z + dz) % NZ],
                lambda x, z, y, c: xr.at[h, (z + dz) % NZ],
                xs.at[h, k], lambda *_: xrr.at[h, k], XP,
            )

    def scatter_z(h):
        add_sib(h, 0)
        for k, dz in enumerate(order):
            slot = (z + dz) % NZ
            n = x * NZ + slot
            over_x[h, dz].recv()
            if dz:
                p[h, c, n] = p[h, c, n] + xr[h, slot]
                over_z[h, dz] = send(
                    p.at[h, c, n], lambda x, z, y, c: rz.at[h, z], zs.at[h, k],
                    lambda x, z, y, c: zr.at[h, z], (0, dz, 0, 0),
                )
            else:
                rz[h, z] = p[h, c, n] + xr[h, slot]

    def gather_z(h):
        total = rz[h, z]
        for dz in Z_NEAR:
            over_z[h, dz].recv()
            total = total + rz[h, (z - dz + NZ) % NZ]
        pf[h, mine] = total
        for k, (dx, dz) in enumerate(((1, 0),) + tuple((0, dz) for dz in Z_NEAR)):
            gather[h, dz] = send(
                pf.at[h, mine], lambda x, z, y, c: pf.at[h, x * NZ + z], ags.at[h, k],
                lambda x, z, y, c: agr.at[h, x * NZ + z], (dx, dz, 0, 0),
            )
        return total

    def forward_x(h):
        for k, dz in enumerate(Z_NEAR):
            gather[h, dz].recv()
            forward[h, dz] = send(
                pf.at[h, x * NZ + (z - dz + NZ) % NZ],
                lambda x, z, y, c: pf.at[h, x * NZ + (z - dz + NZ) % NZ],
                fws.at[h, k],
                lambda x, z, y, c: agr.at[h, x * NZ + (z - dz + NZ) % NZ],
                XP,
            )

    exchange_x(0)
    exchange_x(1)
    grads_in = send(g.at[other], lambda *_: gs, ses.at[0], lambda *_: ser.at[0], SIB)
    scatter_z(0)
    scatter_z(1)
    totals = [gather_z(0)]
    totals.append(gather_z(1))

    first_in.recv()
    second_in.recv()
    one, two, direction = adam(
        scale * jnp.concatenate(totals, axis=1), mo[0].reshape(48, rank), mo[1].reshape(48, rank)
    )
    mres[0] = one.reshape(2, 24, rank)
    mres[1] = two.reshape(2, 24, rank)
    o1[c] = mres[0, c]
    o2[c] = mres[1, c]
    df[mine] = direction
    send(mres.at[0, other], lambda x, z, y, c: o1.at[c], ses.at[3], lambda *_: ser.at[3], SIB)
    send(mres.at[1, other], lambda x, z, y, c: o2.at[c], ses.at[4], lambda *_: ser.at[4], SIB)

    forward_x(0)
    forward_x(1)
    directions = [
        send(
            df.at[mine], lambda x, z, y, c: df.at[x * NZ + z], drs.at[k],
            lambda x, z, y, c: drr.at[z], (0, dz, 0, 0),
        )
        for k, dz in enumerate(Z_NEAR)
    ]

    def q_of(dx, dy):
        return ((x + dx) % NX) * NY + (y + dy) % NY

    over_q, over_z2, gather_z2, gather_q = {}, {}, {}, {}

    def power_part(h):
        gather[h, 0].recv()
        for dz in Z_NEAR:
            forward[h, dz].recv()
        high, low = halves(pf[h].reshape(768, half))
        phl[h, :, 0:half] = high
        phl[h, :, half:rank] = low
        right = phl[h]
        out = dot(g[c], right, ((0,), (0,))) + dot(gs[...], right, ((0,), (0,)))
        pw[h] = (out[:, 0:half] + out[:, half:rank]).reshape(8, 96, half)
        for k, (dx, dy) in enumerate(Q_SEND):
            over_q[h, dx, dy] = send(
                pw.at[h, q_of(dx, dy)], lambda x, z, y, c: r1.at[h, x * NY + y], p1s.at[h, k],
                lambda x, z, y, c: p1r.at[h, x * NY + y], (dx, 0, dy, 0),
            )

    def reduce_q(h):
        part = pw[h, me_q]
        for dx, dy in Q_NEAR:
            over_q[h, dx, dy].recv()
            part = part + r1[h, q_of(dx, NY - dy)]
        for t in range(NZ):
            s2[h, t, 0:12] = part[12 * t : 12 * t + 12]
        for k, dz in enumerate(Z_FAR):
            over_z2[h, dz] = send(
                s2.at[h, (z + dz) % NZ], lambda x, z, y, c: r2.at[h, z], p2s.at[h, k],
                lambda x, z, y, c: p2r.at[h, z], (0, dz, 0, 0),
            )

    def reduce_z(h):
        part = s2[h, z]
        for dz in Z_NEAR:
            over_z2[h, dz].recv()
            part = part + r2[h, (z - dz + NZ) % NZ]
        z2[h, z] = part
        for k, dz in enumerate(Z_FAR):
            gather_z2[h, dz] = send(
                z2.at[h, z], lambda x, z, y, c: z2.at[h, z], q2s.at[h, k],
                lambda x, z, y, c: q2r.at[h, z], (0, dz, 0, 0),
            )

    def spread_q(h):
        for dz in Z_NEAR:
            gather_z2[h, dz].recv()
        for t in range(NZ):
            pwf[h, me_q, 12 * t : 12 * t + 12] = z2[h, t, 0:12]
        for k, (dx, dy) in enumerate(Q_SEND):
            gather_q[h, dx, dy] = send(
                pwf.at[h, me_q], lambda x, z, y, c: pwf.at[h, x * NY + y], q1s.at[h, k],
                lambda x, z, y, c: q1r.at[h, x * NY + y], (dx, 0, dy, 0),
            )

    s2[...] = jnp.zeros_like(s2)
    grads_in.recv()
    first_flows = len(log)
    power_part(0)
    power_part(1)
    reduce_q(0)
    reduce_q(1)
    for item in directions:
        item.recv()
    dir_x = send(
        df.at[column_of(x)], lambda x, z, y, c: df.at[column_of(x)], drs.at[7], lambda *_: drr.at[8], XP
    )
    factor = learn_rate * galore_scale * scale

    def renew(j):
        column = (x + j) % NX
        rows = pl.ds(pl.multiple_of(384 * column, 384), 384)
        dh, dl = halves(df[column_of(column)].reshape(384, rank))
        across = ((1,), (1,))
        update = dot(dh, bh[c], across) + (dot(dh, bl[c], across) + dot(dl, bh[c], across))
        wn[c, rows, :] = (w[rows, :].astype(f32) - factor * update).astype(bf16)
        send(
            wn.at[c, rows],
            lambda x, z, y, c: wn.at[c, pl.ds(pl.multiple_of(384 * ((x + j) % NX), 384), 384)],
            ws.at[j], lambda *_: wr.at[j], SIB,
        )

    reduce_z(0)
    reduce_z(1)
    settle(first_flows)
    renew(0)
    later_flows = len(log)
    spread_q(0)
    spread_q(1)
    dir_x.recv()
    renew(1)
    settle(later_flows)

    for item in gather_q.values():
        item.recv()

    power = jnp.concatenate([pwf[h].reshape(768, half) for h in HALVES], axis=1)
    norm = jnp.sqrt(jnp.sum(power * power))
    iterate = power * (1.0 / (norm + norm_eps))
    it = halves(iterate)
    gram = mm3((it[0].T, it[1].T), it)
    diagonal = (
        lax.broadcasted_iota(jnp.int32, (rank, rank), 0)
        == lax.broadcasted_iota(jnp.int32, (rank, rank), 1)
    )
    mix = None
    for sweep in range(NS_ITERS):
        gh = halves(gram)
        step = coeff_b * gram + coeff_c * mm3(gh, gh)
        step = step + jnp.where(diagonal, coeff_a, 0.0)
        sh = halves(step)
        mix = sh if mix is None else halves(mm3(mix, sh))
        if sweep < NS_ITERS - 1:
            gram = mm3(halves(mm3(gh, sh)), sh)
    for k in range(2):
        rows = pl.ds(384 * k, 384)
        left = halves(iterate[384 * k : 384 * k + 384])
        bn[c, rows, :] = width**0.5 * mm3(left, mix)
        send(bn.at[c, rows], lambda x, z, y, c, rows=rows: bn.at[c, rows], bs.at[k], lambda *_, k=k: br.at[k], SIB)
    finish()


def write_out(wv, bv, v1, v2, wn, bn, o1, o2, sem):
    pairs = [(v1, o1), (v2, o2)]
    pairs += [(wv.at[k // 2, pl.ds(384 * (k % 2), 384)], wn.at[k // 2, pl.ds(384 * (k % 2), 384)]) for k in range(4)]
    pairs += [(bv.at[k], bn.at[k]) for k in range(2)]
    copies = [pltpu.make_async_copy(src, dst, sem.at[k]) for k, (src, dst) in enumerate(pairs)]
    for item in copies:
        item.start()
    for item in copies:
        item.wait()


def body(grads, weights, basis, first, second):
    layers, width, rank = basis.shape
    any_spec = pl.BlockSpec(memory_space=pl.ANY)
    vmem_spec = pl.BlockSpec(memory_space=pltpu.VMEM)
    dma = pltpu.SemaphoreType.DMA
    results = ((weights.shape, bf16), (basis.shape, f32), (first.shape, f32), (second.shape, f32))
    held = pl.pallas_call(
        kernel,
        out_shape=tuple(pltpu.VMEM(shape, dtype) for shape, dtype in results),
        in_specs=[any_spec] * 5,
        out_specs=[vmem_spec] * 4,
        scratch_shapes=[
            pltpu.VMEM((2, 768, 768), bf16),
            pltpu.VMEM((768, 768), bf16),
            pltpu.VMEM((2, 768, 256), f32),
            pltpu.VMEM((2, 768, 256), bf16),
            pltpu.VMEM((2, 768, 256), bf16),
            pltpu.VMEM((768, 768), bf16),
            pltpu.VMEM((2, 2, 16, 48, 128), f32),
            pltpu.VMEM((2, 16, 48, 128), f32),
            pltpu.VMEM((2, 8, 48, 128), f32),
            pltpu.VMEM((2, 8, 48, 128), f32),
            pltpu.VMEM((2, 16, 48, 128), f32),
            pltpu.VMEM((2, 768, 256), bf16),
            pltpu.VMEM((16, 48, 256), f32),
            pltpu.VMEM((2, 2, 24, 256), f32),
            pltpu.VMEM((2, 2, 24, 256), f32),
            pltpu.VMEM((2, 8, 96, 128), f32),
            pltpu.VMEM((2, 8, 96, 128), f32),
            pltpu.VMEM((2, 8, 16, 128), f32),
            pltpu.VMEM((2, 8, 16, 128), f32),
            pltpu.VMEM((2, 8, 16, 128), f32),
            pltpu.VMEM((2, 8, 96, 128), f32),
            dma((7,)),
            dma((2, 2)), dma((2, 2)),
            dma((5,)), dma((5,)),
            dma((2, 8)), dma((2, 8)),
            dma((2, 8)), dma((2, 8)),
            dma((2, 8)), dma((2, 16)), dma((2, 7)),
            dma((8,)), dma((9,)),
            dma((2, 7)), dma((2, 8)),
            dma((2, 7)), dma((2, 8)),
            dma((2, 7)), dma((2, 8)),
            dma((2, 7)), dma((2, 8)),
            dma((2,)), dma((2,)),
            dma((2,)), dma((2,)),
        ],
        name="galore_step",
        compiler_params=pltpu.CompilerParams(
            collective_id=0, has_side_effects=True, vmem_limit_bytes=56 << 20
        ),
    )(grads, weights, basis, first, second)
    return pl.pallas_call(
        write_out,
        out_shape=tuple(jax.ShapeDtypeStruct(shape, dtype) for shape, dtype in results),
        in_specs=[vmem_spec] * 4,
        out_specs=[any_spec] * 4,
        scratch_shapes=[dma((8,))],
        name="write_out",
        compiler_params=pltpu.CompilerParams(vmem_limit_bytes=1 << 20),
    )(*(pltpu.with_memory_space_constraint(item, pltpu.VMEM) for item in held))


def solution(mesh):
    return jax.shard_map(
        body,
        mesh=mesh,
        in_specs=(
            P("shard", "section", "tensor", None),
            P("section", "tensor", None),
            P("section", None, None),
            P("section", ("tensor", "shard"), None),
            P("section", ("tensor", "shard"), None),
        ),
        out_specs=(
            P("section", "tensor", None),
            P("section", None, None),
            P("section", ("tensor", "shard"), None),
            P("section", ("tensor", "shard"), None),
        ),
        check_vma=False,
    )
```

```python
import jax
import jax.numpy as jnp
from jax import lax
from jax.experimental import pallas as pl
from jax.experimental.pallas import tpu as pltpu
from jax.sharding import PartitionSpec as P

NS_ITERS = 3
STEP = 1000

learn_rate = 0.5
galore_scale = 0.25
beta_one = 0.9
beta_two = 0.999
adam_eps = 1e-08
norm_eps = 1e-07
coeff_a = 3.4445
coeff_b = -4.775
coeff_c = 2.0315

f32 = jnp.float32
bf16 = jnp.bfloat16
MESH = pl.DeviceIdType.MESH

NX, NZ, NY = 2, 8, 4
Z_FAR = (4, 3, 5, 2, 6, 1, 7)
Z_NEAR = (1, 7, 2, 6, 3, 5, 4)
Q_NEAR = ((0, 1), (0, 3), (1, 0), (1, 1), (1, 3), (0, 2), (1, 2))
Q_SEND = ((1, 2), (1, 1), (1, 3), (1, 0), (0, 2), (0, 1), (0, 3))


def halves(value):
    high = value.astype(bf16)
    return high, (value - high.astype(f32)).astype(bf16)


def mm(a, b):
    return jnp.dot(a, b, preferred_element_type=f32)


def mm3(a, b):
    (ah, al), (bh, bl) = a, b
    return mm(ah, bh) + (mm(ah, bl) + mm(al, bh))


def adam(reduced, first, second):
    one = beta_one * first + (1.0 - beta_one) * reduced
    two = beta_two * second + (1.0 - beta_two) * reduced * reduced
    corrected_one = one / (1.0 - beta_one**STEP)
    corrected_two = two / (1.0 - beta_two**STEP)
    return one, two, corrected_one / (jnp.sqrt(corrected_two) + adam_eps)


class Flow:
    def __init__(self, me, log, src, dst, send, recv, rel):
        away = {
            "shard": (((me[0] + rel[0]) % NX) * NZ + (me[1] + rel[1]) % NZ) * 2 + (me[3] + rel[3]) % 2,
            "tensor": (me[2] + rel[2]) % NY,
        }
        sizes = (NX, NZ, NY, 2)
        back = tuple(m if r == 0 else (m - r + n) % n for m, r, n in zip(me, rel, sizes))
        self.out = pltpu.make_async_remote_copy(
            src_ref=src, dst_ref=dst(*me), send_sem=send, recv_sem=recv(*me), device_id=away, device_id_type=MESH
        )
        self.back = pltpu.make_async_remote_copy(
            src_ref=dst(*back), dst_ref=dst(*back), send_sem=send, recv_sem=recv(*back),
            device_id=away, device_id_type=MESH,
        )
        self.log = log
        self.waiting = True
        log.append(self)
        self.out.start()

    def recv(self):
        self.back.wait_recv()
        self.waiting = False

    def done(self):
        if self.waiting:
            self.recv()
        self.out.wait_send()


def dot(a, b, dims):
    return lax.dot_general(a, b, (dims, ((), ())), preferred_element_type=f32)


def kernel(
    grads, weights, basis, first, second,
    wn, bn, o1, o2,
    g, gs, b, bh, bl, w, p, ps, xr, rz, pf, phl, df, mo, mres, pw, r1, s2, r2, z2, pwf,
    lsem, sps, spr, ses, ser, xs, xrr, zs, zr, ags, agr, fws, drs, drr,
    p1s, p1r, p2s, p2r, q2s, q2r, q1s, q1r, ws, wr, bs, br,
):
    s = lax.axis_index("shard")
    y = lax.axis_index("tensor")
    x, z, c = s // 16, (s // 2) % 8, s % 2
    me = (x, z, y, c)
    other = 1 - c
    ox = 1 - x
    width, rank = b.shape[1], b.shape[2]
    half = rank // 2
    scale = width ** (-0.5)
    mine = x * NZ + z
    me_q = x * NY + y
    log = []
    SIB, XP = (0, 0, 0, 1), (1, 0, 0, 0)
    HALVES = (0, 1)

    def send(src, dst, ss, rs, rel):
        return Flow(me, log, src, dst, ss, rs, rel)

    def settle(count):
        for item in log[:count]:
            item.done()
        del log[:count]

    def finish():
        settle(len(log))

    barrier = pltpu.get_barrier_semaphore()
    peers = [SIB]
    peers += [(dx, 0, dy, 0) for dx in range(NX) for dy in range(NY) if (dx, dy) != (0, 0)]
    peers += [(0, dz, 0, 0) for dz in range(1, NZ)]
    for dx, dz, dy, dc in peers:
        dev = {"shard": (((x + dx) % NX) * NZ + (z + dz) % NZ) * 2 + (c + dc) % 2, "tensor": (y + dy) % NY}
        pl.semaphore_signal(barrier, 1, device_id=dev, device_id_type=MESH)

    loads = [
        pltpu.make_async_copy(basis.at[other], b.at[other], lsem.at[0]),
        pltpu.make_async_copy(grads.at[0, other], g.at[other], lsem.at[1]),
        pltpu.make_async_copy(basis.at[c], b.at[c], lsem.at[2]),
        pltpu.make_async_copy(grads.at[0, c], g.at[c], lsem.at[3]),
        pltpu.make_async_copy(first.at[c], mo.at[0, c], lsem.at[4]),
        pltpu.make_async_copy(second.at[c], mo.at[1, c], lsem.at[5]),
        pltpu.make_async_copy(weights.at[c], w, lsem.at[6]),
    ]
    for load in loads:
        load.start()

    def column_of(xx):
        return pl.ds(pl.multiple_of(xx * NZ, NZ), NZ)

    def project(layer, column):
        rows = pl.ds(pl.multiple_of(column * 384, 384), 384)
        left = g[layer, rows, :]
        out = mm(left, bh[layer]) + mm(left, bl[layer])
        for h in HALVES:
            p[h, layer, column_of(column)] = out[:, half * h : half * h + half].reshape(NZ, 48, half)

    def split_basis(layer):
        high, low = halves(b[layer])
        bh[layer] = high
        bl[layer] = low

    for k, layer in enumerate((other, c)):
        loads[2 * k].wait()
        split_basis(layer)
        loads[2 * k + 1].wait()
        project(layer, ox)
        project(layer, x)
    for load in loads[4:]:
        load.wait()
    pl.semaphore_wait(barrier, len(peers))

    to_sib = {}
    for h in HALVES:
        for dx in (1, 0):
            to_sib[h, dx] = send(
                p.at[h, other, column_of((x + dx) % NX)],
                lambda x, z, y, c: ps.at[h, column_of((x + dx) % NX)],
                sps.at[h, dx], lambda *_: spr.at[h, dx], SIB,
            )
    first_in = send(first.at[other], lambda x, z, y, c: mo.at[0, c], ses.at[1], lambda *_: ser.at[1], SIB)
    second_in = send(second.at[other], lambda x, z, y, c: mo.at[1, c], ses.at[2], lambda *_: ser.at[2], SIB)

    order = Z_FAR + (0,)

    def add_sib(h, dx):
        to_sib[h, dx].recv()
        rows = column_of((x + dx) % NX)
        p[h, c, rows] = p[h, c, rows] + ps[h, rows]

    over_x, over_z, gather, forward = {}, {}, {}, {}

    def exchange_x(h):
        add_sib(h, 1)
        for k, dz in enumerate(order):
            over_x[h, dz] = send(
                p.at[h, c, ox * NZ + (z + dz) % NZ],
                lambda x, z, y, c: xr.at[h, (z + dz) % NZ],
                xs.at[h, k], lambda *_: xrr.at[h, k], XP,
            )

    def scatter_z(h):
        add_sib(h, 0)
        for k, dz in enumerate(order):
            slot = (z + dz) % NZ
            n = x * NZ + slot
            over_x[h, dz].recv()
            if dz:
                p[h, c, n] = p[h, c, n] + xr[h, slot]
                over_z[h, dz] = send(
                    p.at[h, c, n], lambda x, z, y, c: rz.at[h, z], zs.at[h, k],
                    lambda x, z, y, c: zr.at[h, z], (0, dz, 0, 0),
                )
            else:
                rz[h, z] = p[h, c, n] + xr[h, slot]

    def gather_z(h):
        total = rz[h, z]
        for dz in Z_NEAR:
            over_z[h, dz].recv()
            total = total + rz[h, (z - dz + NZ) % NZ]
        pf[h, mine] = total
        for k, (dx, dz) in enumerate(((1, 0),) + tuple((0, dz) for dz in Z_NEAR)):
            gather[h, dz] = send(
                pf.at[h, mine], lambda x, z, y, c: pf.at[h, x * NZ + z], ags.at[h, k],
                lambda x, z, y, c: agr.at[h, x * NZ + z], (dx, dz, 0, 0),
            )
        return total

    def forward_x(h):
        for k, dz in enumerate(Z_NEAR):
            gather[h, dz].recv()
            forward[h, dz] = send(
                pf.at[h, x * NZ + (z - dz + NZ) % NZ],
                lambda x, z, y, c: pf.at[h, x * NZ + (z - dz + NZ) % NZ],
                fws.at[h, k],
                lambda x, z, y, c: agr.at[h, x * NZ + (z - dz + NZ) % NZ],
                XP,
            )

    exchange_x(0)
    exchange_x(1)
    grads_in = send(g.at[other], lambda *_: gs, ses.at[0], lambda *_: ser.at[0], SIB)
    scatter_z(0)
    scatter_z(1)
    totals = [gather_z(0)]
    totals.append(gather_z(1))

    forward_x(0)
    first_in.recv()
    second_in.recv()
    one, two, direction = adam(
        scale * jnp.concatenate(totals, axis=1), mo[0].reshape(48, rank), mo[1].reshape(48, rank)
    )
    mres[0] = one.reshape(2, 24, rank)
    mres[1] = two.reshape(2, 24, rank)
    o1[c] = mres[0, c]
    o2[c] = mres[1, c]
    df[mine] = direction
    send(mres.at[0, other], lambda x, z, y, c: o1.at[c], ses.at[3], lambda *_: ser.at[3], SIB)
    send(mres.at[1, other], lambda x, z, y, c: o2.at[c], ses.at[4], lambda *_: ser.at[4], SIB)

    forward_x(1)
    def q_of(dx, dy):
        return ((x + dx) % NX) * NY + (y + dy) % NY

    over_q, over_z2, gather_z2, gather_q = {}, {}, {}, {}

    def power_part(h):
        gather[h, 0].recv()
        for dz in Z_NEAR:
            forward[h, dz].recv()
        high, low = halves(pf[h].reshape(768, half))
        phl[h, :, 0:half] = high
        phl[h, :, half:rank] = low
        right = phl[h]
        out = dot(g[c], right, ((0,), (0,))) + dot(gs[...], right, ((0,), (0,)))
        pw[h] = (out[:, 0:half] + out[:, half:rank]).reshape(8, 96, half)
        for k, (dx, dy) in enumerate(Q_SEND):
            over_q[h, dx, dy] = send(
                pw.at[h, q_of(dx, dy)], lambda x, z, y, c: r1.at[h, x * NY + y], p1s.at[h, k],
                lambda x, z, y, c: p1r.at[h, x * NY + y], (dx, 0, dy, 0),
            )

    def reduce_q(h):
        part = pw[h, me_q]
        for dx, dy in Q_NEAR:
            over_q[h, dx, dy].recv()
            part = part + r1[h, q_of(dx, NY - dy)]
        for t in range(NZ):
            s2[h, t, 0:12] = part[12 * t : 12 * t + 12]
        for k, dz in enumerate(Z_FAR):
            over_z2[h, dz] = send(
                s2.at[h, (z + dz) % NZ], lambda x, z, y, c: r2.at[h, z], p2s.at[h, k],
                lambda x, z, y, c: p2r.at[h, z], (0, dz, 0, 0),
            )

    def reduce_z(h):
        part = s2[h, z]
        for dz in Z_NEAR:
            over_z2[h, dz].recv()
            part = part + r2[h, (z - dz + NZ) % NZ]
        z2[h, z] = part
        for k, dz in enumerate(Z_FAR):
            gather_z2[h, dz] = send(
                z2.at[h, z], lambda x, z, y, c: z2.at[h, z], q2s.at[h, k],
                lambda x, z, y, c: q2r.at[h, z], (0, dz, 0, 0),
            )

    def spread_q(h):
        for dz in Z_NEAR:
            gather_z2[h, dz].recv()
        for t in range(NZ):
            pwf[h, me_q, 12 * t : 12 * t + 12] = z2[h, t, 0:12]
        for k, (dx, dy) in enumerate(Q_SEND):
            gather_q[h, dx, dy] = send(
                pwf.at[h, me_q], lambda x, z, y, c: pwf.at[h, x * NY + y], q1s.at[h, k],
                lambda x, z, y, c: q1r.at[h, x * NY + y], (dx, 0, dy, 0),
            )

    s2[...] = jnp.zeros_like(s2)
    grads_in.recv()
    first_flows = len(log)
    power_part(0)
    directions = [
        send(
            df.at[mine], lambda x, z, y, c: df.at[x * NZ + z], drs.at[k],
            lambda x, z, y, c: drr.at[z], (0, dz, 0, 0),
        )
        for k, dz in enumerate(Z_NEAR)
    ]

    power_part(1)
    reduce_q(0)
    reduce_q(1)
    for item in directions:
        item.recv()
    dir_x = send(
        df.at[column_of(x)], lambda x, z, y, c: df.at[column_of(x)], drs.at[7], lambda *_: drr.at[8], XP
    )
    factor = learn_rate * galore_scale * scale

    def renew(j):
        column = (x + j) % NX
        rows = pl.ds(pl.multiple_of(384 * column, 384), 384)
        dh, dl = halves(df[column_of(column)].reshape(384, rank))
        across = ((1,), (1,))
        update = dot(dh, bh[c], across) + (dot(dh, bl[c], across) + dot(dl, bh[c], across))
        wn[c, rows, :] = (w[rows, :].astype(f32) - factor * update).astype(bf16)
        send(
            wn.at[c, rows],
            lambda x, z, y, c: wn.at[c, pl.ds(pl.multiple_of(384 * ((x + j) % NX), 384), 384)],
            ws.at[j], lambda *_: wr.at[j], SIB,
        )

    reduce_z(0)
    reduce_z(1)
    settle(first_flows)
    renew(0)
    later_flows = len(log)
    spread_q(0)
    spread_q(1)
    dir_x.recv()
    renew(1)
    settle(later_flows)

    for item in gather_q.values():
        item.recv()

    power = jnp.concatenate([pwf[h].reshape(768, half) for h in HALVES], axis=1)
    norm = jnp.sqrt(jnp.sum(power * power))
    iterate = power * (1.0 / (norm + norm_eps))
    it = halves(iterate)
    gram = mm3((it[0].T, it[1].T), it)
    diagonal = (
        lax.broadcasted_iota(jnp.int32, (rank, rank), 0)
        == lax.broadcasted_iota(jnp.int32, (rank, rank), 1)
    )
    mix = None
    for sweep in range(NS_ITERS):
        gh = halves(gram)
        step = coeff_b * gram + coeff_c * mm3(gh, gh)
        step = step + jnp.where(diagonal, coeff_a, 0.0)
        sh = halves(step)
        mix = sh if mix is None else halves(mm3(mix, sh))
        if sweep < NS_ITERS - 1:
            gram = mm3(halves(mm3(gh, sh)), sh)
    for k in range(2):
        rows = pl.ds(384 * k, 384)
        left = halves(iterate[384 * k : 384 * k + 384])
        bn[c, rows, :] = width**0.5 * mm3(left, mix)
        send(bn.at[c, rows], lambda x, z, y, c, rows=rows: bn.at[c, rows], bs.at[k], lambda *_, k=k: br.at[k], SIB)
    finish()


def write_out(wv, bv, v1, v2, wn, bn, o1, o2, sem):
    pairs = [(v1, o1), (v2, o2)]
    pairs += [(wv.at[k // 2, pl.ds(384 * (k % 2), 384)], wn.at[k // 2, pl.ds(384 * (k % 2), 384)]) for k in range(4)]
    pairs += [(bv.at[k], bn.at[k]) for k in range(2)]
    copies = [pltpu.make_async_copy(src, dst, sem.at[k]) for k, (src, dst) in enumerate(pairs)]
    for item in copies:
        item.start()
    for item in copies:
        item.wait()


def body(grads, weights, basis, first, second):
    layers, width, rank = basis.shape
    any_spec = pl.BlockSpec(memory_space=pl.ANY)
    vmem_spec = pl.BlockSpec(memory_space=pltpu.VMEM)
    dma = pltpu.SemaphoreType.DMA
    results = ((weights.shape, bf16), (basis.shape, f32), (first.shape, f32), (second.shape, f32))
    held = pl.pallas_call(
        kernel,
        out_shape=tuple(pltpu.VMEM(shape, dtype) for shape, dtype in results),
        in_specs=[any_spec] * 5,
        out_specs=[vmem_spec] * 4,
        scratch_shapes=[
            pltpu.VMEM((2, 768, 768), bf16),
            pltpu.VMEM((768, 768), bf16),
            pltpu.VMEM((2, 768, 256), f32),
            pltpu.VMEM((2, 768, 256), bf16),
            pltpu.VMEM((2, 768, 256), bf16),
            pltpu.VMEM((768, 768), bf16),
            pltpu.VMEM((2, 2, 16, 48, 128), f32),
            pltpu.VMEM((2, 16, 48, 128), f32),
            pltpu.VMEM((2, 8, 48, 128), f32),
            pltpu.VMEM((2, 8, 48, 128), f32),
            pltpu.VMEM((2, 16, 48, 128), f32),
            pltpu.VMEM((2, 768, 256), bf16),
            pltpu.VMEM((16, 48, 256), f32),
            pltpu.VMEM((2, 2, 24, 256), f32),
            pltpu.VMEM((2, 2, 24, 256), f32),
            pltpu.VMEM((2, 8, 96, 128), f32),
            pltpu.VMEM((2, 8, 96, 128), f32),
            pltpu.VMEM((2, 8, 16, 128), f32),
            pltpu.VMEM((2, 8, 16, 128), f32),
            pltpu.VMEM((2, 8, 16, 128), f32),
            pltpu.VMEM((2, 8, 96, 128), f32),
            dma((7,)),
            dma((2, 2)), dma((2, 2)),
            dma((5,)), dma((5,)),
            dma((2, 8)), dma((2, 8)),
            dma((2, 8)), dma((2, 8)),
            dma((2, 8)), dma((2, 16)), dma((2, 7)),
            dma((8,)), dma((9,)),
            dma((2, 7)), dma((2, 8)),
            dma((2, 7)), dma((2, 8)),
            dma((2, 7)), dma((2, 8)),
            dma((2, 7)), dma((2, 8)),
            dma((2,)), dma((2,)),
            dma((2,)), dma((2,)),
        ],
        name="galore_step",
        compiler_params=pltpu.CompilerParams(
            collective_id=0, has_side_effects=True, vmem_limit_bytes=56 << 20
        ),
    )(grads, weights, basis, first, second)
    return pl.pallas_call(
        write_out,
        out_shape=tuple(jax.ShapeDtypeStruct(shape, dtype) for shape, dtype in results),
        in_specs=[vmem_spec] * 4,
        out_specs=[any_spec] * 4,
        scratch_shapes=[dma((8,))],
        name="write_out",
        compiler_params=pltpu.CompilerParams(vmem_limit_bytes=1 << 20),
    )(*(pltpu.with_memory_space_constraint(item, pltpu.VMEM) for item in held))


def solution(mesh):
    return jax.shard_map(
        body,
        mesh=mesh,
        in_specs=(
            P("shard", "section", "tensor", None),
            P("section", "tensor", None),
            P("section", None, None),
            P("section", ("tensor", "shard"), None),
            P("section", ("tensor", "shard"), None),
        ),
        out_specs=(
            P("section", "tensor", None),
            P("section", None, None),
            P("section", ("tensor", "shard"), None),
            P("section", ("tensor", "shard"), None),
        ),
        check_vma=False,
    )
```
